32 devices in a mesh: clip: 2 (over y), tm: 4 (over z), head: 2 (over x), sub: 2 (over core).
Axes of the slice: x: 2, y: 2, z: 4, core: 2. Of those that a mesh axis runs over, the one named last changes fastest.
Arguments:
- queries: bfloat16 [8, 256, 3072], P(('clip', 'tm'), None, ('head', 'sub')), parts along dimension 0, may hold values from -6 to 6, as said below
- keys: bfloat16 [8, 256, 3072], P(('clip', 'tm'), None, ('head', 'sub')), parts along dimension 0, may hold values from -6 to 6, as said below
- values: bfloat16 [8, 256, 3072], P(('clip', 'tm'), None, ('head', 'sub')), parts along dimension 0, may hold values from -6 to 6
- band_table: int32 [4, 4], replicated, may hold values from 0 to 3, as said below
- windows: int32 [7], replicated, may hold values from 1 to 128, as said below
- out_weight: bfloat16 [3072, 3072], P(('head', 'sub')), may hold values from -0.109375 to 0.109375
Outputs:
- mixed: bfloat16 [8, 256, 3072], P(('clip', 'tm'), ('head', 'sub')), parts along dimension 0
The draws below stay inside these ranges and needn't reach their ends.
There are 2 independent parts, one for each index of `clip`. The reference program is written for one: setup_inputs(seed, part) draws one part's arguments, and reference() takes and returns one part's arrays. A program takes and returns all parts, laid end to end along the dimension named above; an argument that names none is the same for every part. Nothing has to cross between parts.
Inputs may be any that keep to these rules, and one draw needn't show every extreme that they name: `queries`: entries of normal law within the range; some rows may be aligned with some key rows. `keys`: entries of normal law within the range; some rows may be aligned with some query rows. `band_table`: Symmetric; 0 exactly on the diagonal; off the diagonal, for frames at distance d it is floor(log2 d) + 1 or one more, never above 6; the pair of frames 0 and 3 takes the one more (up to 6). windows[0] = 128; for k >= 1, windows[k] lies between max(1, 64 // 2**k) and max(that + 1, 128 // 2**k + 1) - 1.
All inputs are finite; a program needn't handle non-finite values.
Results may differ from the reference program's by a relative error of at most 0.015.
Values may be sent and summed in bfloat16 or wider, within the bound.
A program may use at most 64 MiB of HBM per device.

```python
import jax
import jax.numpy as jnp
from jax import lax

D = 3072
HEADS = 24
HEAD = 128
S = 256
NB = 7
FRAMES = 4


def paired_fields(key):
    shape = (FRAMES, S, HEADS * HEAD)
    query = jnp.clip(jax.random.normal(jax.random.fold_in(key, 11), shape, jnp.float32), -6.0, 6.0)
    keyset = jnp.clip(jax.random.normal(jax.random.fold_in(key, 12), shape, jnp.float32), -6.0, 6.0)
    return (query, keyset)


def draw_queries(key, part):
    return paired_fields(key)[0].astype(jnp.bfloat16)


def draw_keys(key, part):
    return paired_fields(key)[1].astype(jnp.bfloat16)


def draw_band_table(key, part):
    index = jnp.arange(FRAMES, dtype=jnp.int32)
    distance = jnp.abs(index[:, None] - index[None, :])
    base = jnp.zeros((FRAMES, FRAMES), jnp.int32)
    for power in range(16):
        base = base + (distance >= 1 << power).astype(jnp.int32)
    jitter = jax.random.randint(jax.random.fold_in(key, 21), (FRAMES, FRAMES), 0, 2).astype(jnp.int32)
    jitter = jnp.triu(jitter, 1)
    jitter = jitter.at[0, FRAMES - 1].set(1)
    jitter = jitter + jnp.transpose(jitter)
    band = jnp.minimum(base + jitter, NB - 1)
    return jnp.where(distance > 0, band, 0).astype(jnp.int32)


def draw_windows(key, part):
    levels = jnp.left_shift(jnp.ones((NB,), jnp.int32), jnp.arange(NB, dtype=jnp.int32))
    lowest = jnp.maximum(1, S // 4 // levels)
    highest = jnp.maximum(lowest + 1, S // 2 // levels + 1)
    spread = jax.random.randint(jax.random.fold_in(key, 31), (NB,), 0, 1 << 20).astype(jnp.int32)
    reach = lowest + spread % (highest - lowest)
    reach = reach.at[0].set(S // 2)
    return reach.astype(jnp.int32)


def block_levels(key, extent, pieces, smallest, high):
    level = 1.0
    for axis_at, blocks in pieces:
        steps = jax.random.uniform(jax.random.fold_in(jax.random.fold_in(key, 6), axis_at), (blocks,), jnp.float32, smallest / len(pieces), high / len(pieces))
        level = level * jnp.repeat(jnp.exp(steps), extent[axis_at] // blocks).reshape((-1,) + (1,) * (len(extent) - 1 - axis_at))
    return level


def scatter_about(stream_key, extent, scale, limit, cuts=(), kind=jnp.bfloat16):
    gain = block_levels(stream_key, extent, cuts, -0.22, 0.18) if cuts else 1.0
    drawn = jax.random.normal(stream_key, extent, jnp.float32) * scale * gain
    return jnp.minimum(jnp.maximum(drawn, -limit), limit).astype(kind)


def setup_inputs(seed: int = 0, part: int = 0) -> dict:
    key_list = jax.random.split(jax.random.key(seed), 7)
    own_keys = jax.random.split(jax.random.fold_in(key_list[6], part), 7)
    queries = draw_queries(jax.random.fold_in(jax.random.fold_in(key_list[6], part), 71), part)
    keys = draw_keys(jax.random.fold_in(jax.random.fold_in(key_list[6], part), 71), part)
    values = scatter_about(own_keys[2], (FRAMES, S, HEADS * HEAD), 1.0, 6.0, ((0, 4), (2, 4)))
    band_table = draw_band_table(jax.random.fold_in(key_list[6], 71), part)
    windows = draw_windows(jax.random.fold_in(key_list[6], 71), part)
    out_weight = scatter_about(key_list[5], (HEADS * HEAD, D), (HEADS * HEAD) ** -0.5, 0.109375, ((0, 4),))
    return {"queries": queries, "keys": keys, "values": values, "band_table": band_table, "windows": windows, "out_weight": out_weight}


def reference(queries, keys, values, band_table, windows, out_weight):
    heads = HEADS
    scale = HEAD ** -0.5
    key_all = keys.reshape(FRAMES * S, heads, HEAD).astype(jnp.float32)
    value_all = values.reshape(FRAMES * S, heads, HEAD).astype(jnp.float32)
    places = jnp.arange(S, dtype=jnp.int32)
    key_places = jnp.tile(places, FRAMES)
    key_frames = jnp.repeat(jnp.arange(FRAMES, dtype=jnp.int32), S)

    def one_frame(frame):
        query = lax.dynamic_index_in_dim(queries, frame, 0, keepdims=False)
        query = query.reshape(S, heads, HEAD).astype(jnp.float32)
        reach = windows[band_table[frame]]
        allowed = jnp.abs(places[:, None] - key_places[None, :]) <= reach[key_frames][None, :]
        scores = jnp.einsum("phd,qhd->hpq", query, key_all, precision=lax.Precision.HIGHEST) * scale
        masked = jnp.where(allowed[None], scores, jnp.float32(-1e30))
        top = jnp.max(masked, axis=-1, keepdims=True)
        weights = jnp.where(allowed[None], jnp.exp(scores - top), jnp.float32(0.0))
        total = jnp.sum(weights, axis=-1)
        rounded = lax.optimization_barrier(weights.astype(jnp.bfloat16)).astype(jnp.float32)
        numer = jnp.einsum("hpq,qhd->phd", rounded, value_all, precision=lax.Precision.HIGHEST)
        attended = numer / jnp.transpose(total)[:, :, None]
        return attended.reshape(S, heads * HEAD).astype(jnp.bfloat16)

    attended = lax.map(one_frame, jnp.arange(FRAMES, dtype=jnp.int32))
    mixed = jnp.dot(attended.reshape(FRAMES * S, heads * HEAD), out_weight, preferred_element_type=jnp.float32)
    return mixed.astype(jnp.bfloat16).reshape(FRAMES, S, D)
```

```python
import functools
import math

import jax
import jax.numpy as jnp
from jax import lax
from jax.experimental import pallas as pl
from jax.experimental.pallas import tpu as pltpu
from jax.sharding import PartitionSpec as P

HEAD = 128
MESH = pl.DeviceIdType.MESH


def local(queries, keys, values, band_table, windows, out_weight):
    frames, length, width = queries.shape
    heads = width // HEAD
    scale = HEAD ** (-0.5)
    here = lax.axis_index("tm") * frames
    query = queries[0].reshape(length, heads, HEAD)
    places = lax.iota(jnp.int32, length)
    gap = jnp.abs(places[:, None] - places[None, :])

    def absorb(carry, key_frame, value_frame, frame, usable):
        peak, total, numer = carry
        reach = windows[band_table[here, frame]]
        allowed = (gap <= reach)[None] & usable
        scores = (
            jnp.einsum(
                "phd,qhd->hpq",
                query,
                key_frame.reshape(length, heads, HEAD),
                preferred_element_type=jnp.float32,
            )
            * scale
        )
        masked = jnp.where(allowed, scores, jnp.float32(-1e30))
        top = jnp.maximum(peak, jnp.max(masked, axis=-1))
        weights = jnp.where(allowed, jnp.exp(scores - top[:, :, None]), jnp.float32(0.0))
        shrink = jnp.exp(peak - top)
        total = total * shrink + jnp.sum(weights, axis=-1)
        added = jnp.einsum(
            "hpq,qhd->phd",
            weights.astype(jnp.bfloat16),
            value_frame.reshape(length, heads, HEAD),
            preferred_element_type=jnp.float32,
        )
        numer = numer * jnp.transpose(shrink)[:, :, None] + added
        return (top, total, numer)

    carry = (
        jnp.full((heads, length), -1e30, jnp.float32),
        jnp.zeros((heads, length), jnp.float32),
        jnp.zeros((length, heads, HEAD), jnp.float32),
    )
    skipped = -1
    state = carry
    key_part = lax.all_gather(keys, "tm", axis=0, tiled=True)
    value_part = lax.all_gather(values, "tm", axis=0, tiled=True)

    def advance(inner, item):
        key_frame, value_frame, offset = item
        usable = jnp.abs(offset - here) > skipped
        return (absorb(inner, key_frame, value_frame, offset, usable), None)

    state, unused = lax.scan(
        advance, state, (key_part, value_part, lax.iota(jnp.int32, key_part.shape[0]))
    )
    carry = state
    peak, total, numer = carry
    attended = (
        (numer / jnp.transpose(total)[:, :, None]).astype(jnp.bfloat16).reshape(length, width)
    )
    mixed = lax.psum_scatter(
        jnp.dot(attended, out_weight, preferred_element_type=jnp.float32).astype(jnp.bfloat16),
        ("head", "sub"),
        scatter_dimension=0,
        tiled=True,
    )
    return mixed[None]


def fused_kernel(
    n, pieces, chunks, q_hbm, k_hbm, v_hbm, band_hbm, windows_hbm, w_hbm, out_ref,
    band, windows, asked_a, asked_b, buf, weight, done_a, done_b, att,
    send_a, recv_a, send_b, recv_b, acc, own, known,
    in_send, in_recv_a, in_recv_b, back_send_a, back_recv_a, back_send_b, back_recv_b,
    a_send, a_recv, b_send, b_recv, w_sem, table_sem,
):
    frame = lax.axis_index("tm")
    row = lax.axis_index("head")
    core = lax.axis_index("sub")
    length = k_hbm.shape[1]
    block = length // 4
    slab = block // pieces
    heads = 2 * n - 2
    half = n // 2
    owner = [(h + 1) // 2 for h in range(heads)]
    slot = [1 if h > 0 and h % 2 == 0 else 0 for h in range(heads)]
    factor = HEAD ** (-0.5) * math.log2(math.e)
    ahead = min(2, pieces)

    def inner(z):
        return z + 1 if z < half else z - 1

    def outward(z):
        return list(range(z - 1, -1, -1)) if z < half else list(range(z + 1, n))

    def beyond(z):
        return list(range(z + 2, n)) if z < half else list(range(z - 2, -1, -1))

    def owned(z, s):
        return [h for h in range(heads) if owner[h] == z and slot[h] == s]

    def ends(h, a):
        columns = slice(h * HEAD, (h + 1) * HEAD)
        if a < 2:
            return (k_hbm, v_hbm)[a].at[0, :, columns], buf.at[slot[h], a, frame]
        if slot[h]:
            return q_hbm.at[:, :, columns], asked_a.at[frame]
        p = a - 2
        return q_hbm.at[:, p * slab : (p + 1) * slab, columns], asked_b.at[p, frame]

    def landed(h, a):
        return (in_recv_a if slot[h] else in_recv_b).at[a, frame]

    def parts_of(h):
        return 3 if slot[h] else 2 + pieces

    def outgoing(h, a):
        source, target = ends(h, a)
        return pltpu.make_async_remote_copy(
            src_ref=source,
            dst_ref=target,
            send_sem=in_send.at[h, a],
            recv_sem=landed(h, a),
            device_id={"tm": owner[h]},
            device_id_type=MESH,
        )

    def send(some):
        for h in some:
            for a in (0, 2, 1) if slot[h] else (0, 2, 1, *range(3, 2 + ahead)):
                outgoing(h, a).start()

    def tell(z, w):
        pl.semaphore_signal(known.at[w], inc=1, device_id={"tm": z}, device_id_type=MESH)

    def enter(z):
        barrier = pltpu.get_barrier_semaphore()
        middle = z in (half - 1, half)
        out = outward(z)
        for w in ([inner(z)] if middle else []) + out[:1]:
            pl.semaphore_signal(barrier, inc=1, device_id={"tm": w}, device_id_type=MESH)
        pl.semaphore_signal(barrier, inc=1, device_id={"head": 1 - row}, device_id_type=MESH)
        pl.semaphore_signal(barrier, inc=1, device_id={"sub": 1 - core}, device_id_type=MESH)
        pl.semaphore_wait(barrier, 3)
        if not middle:
            tell(inner(z), z)
        send(owned(inner(z), 1))
        if middle:
            send(owned(inner(z), 0))
        for w in out:
            pl.semaphore_wait(known.at[w], 1)
            tell(inner(z), w)
            if w == out[0]:
                tell(w, inner(z))
            send(owned(w, 1) + owned(w, 0))
        for w in beyond(z):
            pl.semaphore_wait(known.at[w], 1)
            if out:
                tell(out[0], w)
            send(owned(w, 1) + owned(w, 0))
        if not middle:
            send(owned(inner(z), 0))
        for h in owned(z, 1) + owned(z, 0):
            for a in range(parts_of(h)):
                source, target = ends(h, a)
                pltpu.make_async_copy(source, target, landed(h, a)).start()

    for z in range(n):
        @pl.when(frame == z)
        def _():
            enter(z)

    load_weight = pltpu.make_async_copy(w_hbm, weight, w_sem)
    load_weight.start()
    tables = (
        pltpu.make_async_copy(band_hbm, band, table_sem.at[0]),
        pltpu.make_async_copy(windows_hbm, windows, table_sem.at[1]),
    )
    for table in tables:
        table.start()
    for table in tables:
        table.wait()

    def returning_a(h, i):
        return pltpu.make_async_remote_copy(
            src_ref=done_a.at[i],
            dst_ref=att.at[:, :, pl.ds(pl.multiple_of(h * HEAD, HEAD), HEAD)],
            send_sem=back_send_a.at[i],
            recv_sem=back_recv_a.at[h],
            device_id={"tm": i},
            device_id_type=MESH,
        )

    def returning_b(h, p, i):
        return pltpu.make_async_remote_copy(
            src_ref=done_b.at[p, i],
            dst_ref=att.at[
                :, p * slab : (p + 1) * slab, pl.ds(pl.multiple_of(h * HEAD, HEAD), HEAD)
            ],
            send_sem=back_send_b.at[p, i],
            recv_sem=back_recv_b.at[p, h],
            device_id={"tm": i},
            device_id_type=MESH,
        )

    def weigh(s, query, masked):
        scores = []
        for j in range(n):
            score = lax.dot_general(
                query, buf[s, 0, j], (((1,), (1,)), ((), ())), preferred_element_type=jnp.float32
            )
            scores.append(masked(j, score))
        top = scores[0]
        for score in scores[1:]:
            top = jnp.maximum(top, score)
        top = jnp.max(top, axis=-1, keepdims=True)
        total = None
        numer = None
        for j in range(n):
            part = jnp.exp2((scores[j] - top) * factor)
            product = jnp.dot(
                part.astype(jnp.bfloat16), buf[s, 1, j], preferred_element_type=jnp.float32
            )
            total = part if total is None else total + part
            numer = product if numer is None else numer + product
        return (numer / jnp.sum(total, axis=-1, keepdims=True)).astype(jnp.bfloat16)

    second = 2 * frame
    first = 2 * frame - (frame + n - 1) // n
    both = jnp.logical_and(frame > 0, frame < n - 1)
    column = lax.broadcasted_iota(jnp.int32, (length, length), 1)
    gap_a = jnp.abs(lax.broadcasted_iota(jnp.int32, (length, length), 0) - column)

    @pl.when(both)
    def _():
        for j in range(n):
            for a in range(2):
                here = buf.at[1, a, j]
                pltpu.make_async_copy(here, here, in_recv_a.at[a, j]).wait()
            here = asked_a.at[j]
            pltpu.make_async_copy(here, here, in_recv_a.at[2, j]).wait()

        def one(step, carry):
            i = lax.rem(frame + 1 + step, n)

            def masked(j, score):
                return jnp.where(gap_a <= windows[band[i, j]], score, jnp.float32(-1e30))

            result = weigh(1, asked_a[i].reshape(length, HEAD), masked)
            result = result.reshape(4, block, HEAD)

            @pl.when(i != frame)
            def _():
                done_a[i] = result
                returning_a(second, i).start()

            @pl.when(i == frame)
            def _():
                att[:, :, pl.ds(pl.multiple_of(second * HEAD, HEAD), HEAD)] = result

            return carry

        lax.fori_loop(0, n, one, 0)

    height = 4 * slab
    spot = lax.broadcasted_iota(jnp.int32, (height, length), 0)
    spot = (spot // slab) * block + lax.rem(spot, slab)
    spot = spot - lax.broadcasted_iota(jnp.int32, (height, length), 1)

    def more(p):
        for z in range(n):
            @pl.when(frame == z)
            def _():
                for w in beyond(z)[::-1] + outward(z) + [inner(z)]:
                    for h in owned(w, 0):
                        outgoing(h, 2 + p).start()

    def attend(p):
        for j in range(n):
            for a in range(2) if p == 0 else ():
                here = buf.at[0, a, j]
                pltpu.make_async_copy(here, here, in_recv_b.at[a, j]).wait()
            here = asked_b.at[p, j]
            pltpu.make_async_copy(here, here, in_recv_b.at[2 + p, j]).wait()
        gap = jnp.abs(spot + p * slab)

        def masked(j, score):
            return jnp.concatenate(
                [
                    jnp.where(
                        gap <= windows[band[i, j]],
                        score[i * height : (i + 1) * height],
                        jnp.float32(-1e30),
                    )
                    for i in range(n)
                ],
                axis=0,
            )

        result = weigh(0, asked_b[p].reshape(n * height, HEAD), masked)
        for i in range(n):
            mine = result[i * height : (i + 1) * height].reshape(4, slab, HEAD)

            @pl.when(i != frame)
            def _():
                done_b[p, i] = mine
                returning_b(first, p, i).start()

            @pl.when(i == frame)
            def _():
                att[
                    :, p * slab : (p + 1) * slab, pl.ds(pl.multiple_of(first * HEAD, HEAD), HEAD)
                ] = mine

    width = weight.shape[1] // chunks

    def give_a(p, c):
        return pltpu.make_async_remote_copy(
            src_ref=send_a.at[p, c], dst_ref=recv_a.at[p, c],
            send_sem=a_send.at[p, c], recv_sem=a_recv.at[p, c],
            device_id={"sub": 1 - core}, device_id_type=MESH,
        )

    def give_b(p, c):
        return pltpu.make_async_remote_copy(
            src_ref=send_b.at[p, c], dst_ref=recv_b.at[p, c],
            send_sem=b_send.at[p, c], recv_sem=b_recv.at[p, c],
            device_id={"head": 1 - row}, device_id_type=MESH,
        )

    def project(p):
        for h in range(heads):
            if slot[h] and p > 0:
                continue

            @pl.when(frame != owner[h])
            def _():
                columns = slice(h * HEAD, (h + 1) * HEAD)
                if slot[h]:
                    here = att.at[:, :, columns]
                    pltpu.make_async_copy(here, here, back_recv_a.at[h]).wait()
                else:
                    here = att.at[:, p * slab : (p + 1) * slab, columns]
                    pltpu.make_async_copy(here, here, back_recv_b.at[p, h]).wait()

        tokens = jnp.concatenate(
            [
                att[r * 2 + who, p * slab : (p + 1) * slab, :]
                for who in (1 - core, core)
                for r in (row, 1 - row)
            ],
            axis=0,
        )
        for c in range(chunks):
            share = jnp.dot(
                tokens, weight[:, c * width : (c + 1) * width], preferred_element_type=jnp.float32
            )
            send_a[p, c] = share[: 2 * slab].astype(jnp.bfloat16)
            give_a(p, c).start()
            own[c] = share[2 * slab :]

    def pair(p):
        for c in range(chunks):
            give_a(p, c).wait_recv()
            both_cores = own[c] + recv_a[p, c].astype(jnp.float32)
            send_b[p, c] = both_cores[slab:].astype(jnp.bfloat16)
            give_b(p, c).start()
            acc[p, c] = both_cores[:slab]

    def finish(p):
        for c in range(chunks):
            give_b(p, c).wait_recv()
            out_ref[p * slab : (p + 1) * slab, c * width : (c + 1) * width] = (
                acc[p, c] + recv_b[p, c].astype(jnp.float32)
            ).astype(jnp.bfloat16)

    for p in range(pieces):
        if p + ahead < pieces:
            more(p + ahead)
        attend(p)
        if p == 1:
            load_weight.wait()
        if p > 1:
            pair(p - 2)
        if p > 0:
            project(p - 1)
    pair(pieces - 2)
    for p in range(pieces - 2):
        finish(p)
    project(pieces - 1)
    finish(pieces - 2)
    pair(pieces - 1)
    finish(pieces - 1)

    for p in range(pieces):
        for c in range(chunks):
            give_a(p, c).wait_send()
            give_b(p, c).wait_send()
    for h in range(heads):

        @pl.when(frame != owner[h])
        def _():
            for a in range(parts_of(h)):
                outgoing(h, a).wait_send()

    for i in range(n):

        @pl.when(i != frame)
        def _():
            for p in range(pieces):
                returning_b(first, p, i).wait_send()

        @pl.when(jnp.logical_and(both, i != frame))
        def _():
            returning_a(second, i).wait_send()


def fused(n, queries, keys, values, band_table, windows, out_weight):
    length, width = queries.shape[1:]
    columns = out_weight.shape[1]
    heads = width // HEAD
    block = length // 4
    chunks = 2
    pieces = 4
    slab = block // pieces
    part = columns // chunks
    anywhere = pl.BlockSpec(memory_space=pl.ANY)
    dma = pltpu.SemaphoreType.DMA
    arrays = (queries.reshape(4, block, width), keys, values, band_table, windows, out_weight)
    mixed = pl.pallas_call(
        functools.partial(fused_kernel, n, pieces, chunks),
        out_shape=pltpu.VMEM((block, columns), jnp.bfloat16),
        in_specs=[anywhere] * 6,
        out_specs=pl.BlockSpec(memory_space=pltpu.VMEM),
        scratch_shapes=[
            pltpu.SMEM(band_table.shape, jnp.int32),
            pltpu.SMEM(windows.shape, jnp.int32),
            pltpu.VMEM((n, 4, block, HEAD), jnp.bfloat16),
            pltpu.VMEM((pieces, n, 4, slab, HEAD), jnp.bfloat16),
            pltpu.VMEM((2, 2, n, length, HEAD), jnp.bfloat16),
            pltpu.VMEM(out_weight.shape, jnp.bfloat16),
            pltpu.VMEM((n, 4, block, HEAD), jnp.bfloat16),
            pltpu.VMEM((pieces, n, 4, slab, HEAD), jnp.bfloat16),
            pltpu.VMEM((4, block, width), jnp.bfloat16),
            pltpu.VMEM((pieces, chunks, 2 * slab, part), jnp.bfloat16),
            pltpu.VMEM((pieces, chunks, 2 * slab, part), jnp.bfloat16),
            pltpu.VMEM((pieces, chunks, slab, part), jnp.bfloat16),
            pltpu.VMEM((pieces, chunks, slab, part), jnp.bfloat16),
            pltpu.VMEM((pieces, chunks, slab, part), jnp.float32),
            pltpu.VMEM((chunks, 2 * slab, part), jnp.float32),
            pltpu.SemaphoreType.REGULAR((n,)),
            dma((heads, 2 + pieces)),
            dma((3, n)),
            dma((2 + pieces, n)),
            dma((n,)),
            dma((heads,)),
            dma((pieces, n)),
            dma((pieces, heads)),
            dma((pieces, chunks)),
            dma((pieces, chunks)),
            dma((pieces, chunks)),
            dma((pieces, chunks)),
            dma,
            dma((2,)),
        ],
        compiler_params=pltpu.CompilerParams(
            collective_id=0, has_side_effects=True, vmem_limit_bytes=60 * 1024 * 1024
        ),
    )(*[pltpu.with_memory_space_constraint(x, pltpu.HBM) for x in arrays])
    return mixed[None]


def solution(mesh):
    n = mesh.shape["tm"]

    def step(queries, keys, values, band_table, windows, out_weight):
        paired = mesh.shape["head"] == 2 and mesh.shape["sub"] == 2
        fits = queries.shape[0] == 1 and queries.shape[1] % 256 == 0
        if n > 2 and paired and fits and queries.shape[2] == (2 * n - 2) * HEAD:
            return fused(n, queries, keys, values, band_table, windows, out_weight)
        return local(queries, keys, values, band_table, windows, out_weight)

    return jax.shard_map(
        step,
        mesh=mesh,
        in_specs=(
            P(("clip", "tm"), None, ("head", "sub")),
            P(("clip", "tm"), None, ("head", "sub")),
            P(("clip", "tm"), None, ("head", "sub")),
            P(),
            P(),
            P(("head", "sub"), None),
        ),
        out_specs=P(("clip", "tm"), ("head", "sub"), None),
        check_vma=False,
    )
```

```python
import functools
import math

import jax
import jax.numpy as jnp
from jax import lax
from jax.experimental import pallas as pl
from jax.experimental.pallas import tpu as pltpu
from jax.sharding import PartitionSpec as P

HEAD = 128
MESH = pl.DeviceIdType.MESH


def local(queries, keys, values, band_table, windows, out_weight):
    frames, length, width = queries.shape
    heads = width // HEAD
    scale = HEAD ** (-0.5)
    here = lax.axis_index("tm") * frames
    query = queries[0].reshape(length, heads, HEAD)
    places = lax.iota(jnp.int32, length)
    gap = jnp.abs(places[:, None] - places[None, :])

    def absorb(carry, key_frame, value_frame, frame, usable):
        peak, total, numer = carry
        reach = windows[band_table[here, frame]]
        allowed = (gap <= reach)[None] & usable
        scores = (
            jnp.einsum(
                "phd,qhd->hpq",
                query,
                key_frame.reshape(length, heads, HEAD),
                preferred_element_type=jnp.float32,
            )
            * scale
        )
        masked = jnp.where(allowed, scores, jnp.float32(-1e30))
        top = jnp.maximum(peak, jnp.max(masked, axis=-1))
        weights = jnp.where(allowed, jnp.exp(scores - top[:, :, None]), jnp.float32(0.0))
        shrink = jnp.exp(peak - top)
        total = total * shrink + jnp.sum(weights, axis=-1)
        added = jnp.einsum(
            "hpq,qhd->phd",
            weights.astype(jnp.bfloat16),
            value_frame.reshape(length, heads, HEAD),
            preferred_element_type=jnp.float32,
        )
        numer = numer * jnp.transpose(shrink)[:, :, None] + added
        return (top, total, numer)

    carry = (
        jnp.full((heads, length), -1e30, jnp.float32),
        jnp.zeros((heads, length), jnp.float32),
        jnp.zeros((length, heads, HEAD), jnp.float32),
    )
    skipped = -1
    state = carry
    key_part = lax.all_gather(keys, "tm", axis=0, tiled=True)
    value_part = lax.all_gather(values, "tm", axis=0, tiled=True)

    def advance(inner, item):
        key_frame, value_frame, offset = item
        usable = jnp.abs(offset - here) > skipped
        return (absorb(inner, key_frame, value_frame, offset, usable), None)

    state, unused = lax.scan(
        advance, state, (key_part, value_part, lax.iota(jnp.int32, key_part.shape[0]))
    )
    carry = state
    peak, total, numer = carry
    attended = (
        (numer / jnp.transpose(total)[:, :, None]).astype(jnp.bfloat16).reshape(length, width)
    )
    mixed = lax.psum_scatter(
        jnp.dot(attended, out_weight, preferred_element_type=jnp.float32).astype(jnp.bfloat16),
        ("head", "sub"),
        scatter_dimension=0,
        tiled=True,
    )
    return mixed[None]


def fused_kernel(
    n, chunks, q_hbm, k_hbm, v_hbm, band_hbm, windows_hbm, w_hbm, out_ref,
    band, windows, asked, buf, weight, done, att, send_a, recv_a, send_b, recv_b, own, known,
    in_send, in_recv, back_send, back_recv, a_send, a_recv, b_send, b_recv, w_sem, table_sem,
):
    frame = lax.axis_index("tm")
    row = lax.axis_index("head")
    core = lax.axis_index("sub")
    length = k_hbm.shape[1]
    block = length // 4
    slab = block // 2
    pieces = 4
    heads = 2 * n - 2
    half = n // 2
    owner = [(h + 1) // 2 for h in range(heads)]
    slot = [1 if h > 0 and h % 2 == 0 else 0 for h in range(heads)]
    factor = HEAD ** (-0.5) * math.log2(math.e)
    ahead = 2

    def inner(z):
        return z + 1 if z < half else z - 1

    def outward(z):
        return list(range(z - 1, -1, -1)) if z < half else list(range(z + 1, n))

    def beyond(z):
        return list(range(z + 2, n)) if z < half else list(range(z - 2, -1, -1))

    def owned(z):
        return [h for h in range(heads) if owner[h] == z and slot[h]] + [
            h for h in range(heads) if owner[h] == z and not slot[h]
        ]

    def piece(ref, p, columns):
        if p < 2:
            return ref.at[pl.ds(2 * (1 - row), 2), p, :, columns]
        return ref.at[2 * row + (1 - core if p == 2 else core), :, :, columns]

    def ends(h, a):
        columns = slice(h * HEAD, (h + 1) * HEAD)
        if a < 2:
            return (k_hbm, v_hbm)[a].at[0, :, columns], buf.at[slot[h], a, frame]
        return piece(q_hbm, a - 2, columns), asked.at[slot[h], a - 2, frame]

    def outgoing(h, a):
        source, target = ends(h, a)
        return pltpu.make_async_remote_copy(
            src_ref=source,
            dst_ref=target,
            send_sem=in_send.at[h, a],
            recv_sem=in_recv.at[slot[h], a, frame],
            device_id={"tm": owner[h]},
            device_id_type=MESH,
        )

    def give(some):
        for h in some:
            for a in range(2):
                outgoing(h, a).start()

    def ask(z, p):
        near = [inner(z)] if z in (half - 1, half) else []
        far = [inner(z)] if z not in (half - 1, half) else []
        for w in near + beyond(z) + far + outward(z):
            for h in owned(w):
                outgoing(h, 2 + p).start()

    def tell(z, w):
        pl.semaphore_signal(known.at[w], inc=1, device_id={"tm": z}, device_id_type=MESH)

    def enter(z):
        barrier = pltpu.get_barrier_semaphore()
        middle = z in (half - 1, half)
        out = outward(z)
        for w in ([inner(z)] if middle else []) + out[:1]:
            pl.semaphore_signal(barrier, inc=1, device_id={"tm": w}, device_id_type=MESH)
        pl.semaphore_signal(barrier, inc=1, device_id={"head": 1 - row}, device_id_type=MESH)
        pl.semaphore_signal(barrier, inc=1, device_id={"sub": 1 - core}, device_id_type=MESH)
        pl.semaphore_wait(barrier, 3)
        if not middle:
            tell(inner(z), z)
        close = owned(inner(z))
        if middle:
            give(close)
        else:
            outgoing(close[0], 0).start()
        for w in out:
            pl.semaphore_wait(known.at[w], 1)
            tell(inner(z), w)
            if w == out[0]:
                tell(w, inner(z))
            give(owned(w))
        for w in beyond(z):
            pl.semaphore_wait(known.at[w], 1)
            if out:
                tell(out[0], w)
            give(owned(w))
        if not middle:
            outgoing(close[0], 1).start()
            give(close[1:])
        ask(z, 0)

        @pl.when(core == 0)
        def _():
            for p in range(1, ahead):
                ask(z, p)

        for h in owned(z):
            for a in range(2 + pieces):
                source, target = ends(h, a)
                pltpu.make_async_copy(source, target, in_recv.at[slot[h], a, frame]).start()

    for z in range(n):
        @pl.when(frame == z)
        def _():
            enter(z)

    load_weight = pltpu.make_async_copy(w_hbm, weight, w_sem)
    load_weight.start()
    tables = (
        pltpu.make_async_copy(band_hbm, band, table_sem.at[0]),
        pltpu.make_async_copy(windows_hbm, windows, table_sem.at[1]),
    )
    for table in tables:
        table.start()
    for table in tables:
        table.wait()

    def returning(s, h, p, i):
        return pltpu.make_async_remote_copy(
            src_ref=done.at[s, p, i],
            dst_ref=piece(att, p, pl.ds(pl.multiple_of(h * HEAD, HEAD), HEAD)),
            send_sem=back_send.at[s, p, i],
            recv_sem=back_recv.at[p, h],
            device_id={"tm": i},
            device_id_type=MESH,
        )

    def weigh(s, query, masked):
        scores = []
        for j in range(n):
            score = lax.dot_general(
                query, buf[s, 0, j], (((1,), (1,)), ((), ())), preferred_element_type=jnp.float32
            )
            scores.append(masked(j, score))
        top = scores[0]
        for score in scores[1:]:
            top = jnp.maximum(top, score)
        top = jnp.max(top, axis=-1, keepdims=True)
        total = None
        numer = None
        for j in range(n):
            part = jnp.exp2((scores[j] - top) * factor)
            product = jnp.dot(
                part.astype(jnp.bfloat16), buf[s, 1, j], preferred_element_type=jnp.float32
            )
            total = part if total is None else total + part
            numer = product if numer is None else numer + product
        return (numer / jnp.sum(total, axis=-1, keepdims=True)).astype(jnp.bfloat16)

    second = 2 * frame
    first = 2 * frame - (frame + n - 1) // n
    both = jnp.logical_and(frame > 0, frame < n - 1)
    height = 2 * slab
    line = lax.broadcasted_iota(jnp.int32, (height, length), 0)
    column = lax.broadcasted_iota(jnp.int32, (height, length), 1)

    def away(p):
        if p < 2:
            spot = (line // slab) * block + lax.rem(line, slab)
            start = 2 * (1 - row) * block + p * slab
        else:
            spot = line
            start = (2 * row + (1 - core if p == 2 else core)) * block
        return jnp.abs(spot - column + start)

    def more(p):
        for z in range(n):
            @pl.when(frame == z)
            def _():
                ask(z, p)

    def arrive(s, p):
        for j in range(n):
            for a in range(2) if p == 0 else ():
                here = buf.at[s, a, j]
                pltpu.make_async_copy(here, here, in_recv.at[s, a, j]).wait()
            here = asked.at[s, p, j]
            pltpu.make_async_copy(here, here, in_recv.at[s, 2 + p, j]).wait()

    def attend(s, h, p):
        gap = away(p)

        def masked(j, score):
            return jnp.concatenate(
                [
                    jnp.where(
                        gap <= windows[band[i, j]],
                        score[i * height : (i + 1) * height],
                        jnp.float32(-1e30),
                    )
                    for i in range(n)
                ],
                axis=0,
            )

        result = weigh(s, asked[s, p].reshape(n * height, HEAD), masked)
        for i in range(n):
            mine = result[i * height : (i + 1) * height].reshape(2, slab, HEAD)

            @pl.when(i != frame)
            def _():
                done[s, p, i] = mine
                returning(s, h, p, i).start()

            @pl.when(i == frame)
            def _():
                piece(att, p, pl.ds(pl.multiple_of(h * HEAD, HEAD), HEAD))[...] = mine

    width = weight.shape[1] // chunks

    def give_a(p, c):
        lines = slice(0, slab if p < 2 else block)
        return pltpu.make_async_remote_copy(
            src_ref=send_a.at[p, c, lines], dst_ref=recv_a.at[p, c, lines],
            send_sem=a_send.at[p, c], recv_sem=a_recv.at[p, c],
            device_id={"sub": 1 - core}, device_id_type=MESH,
        )

    def give_b(p, c):
        return pltpu.make_async_remote_copy(
            src_ref=send_b.at[p, c], dst_ref=recv_b.at[p, c],
            send_sem=b_send.at[p, c], recv_sem=b_recv.at[p, c],
            device_id={"head": 1 - row}, device_id_type=MESH,
        )

    def returned(p):
        for h in range(heads):

            @pl.when(frame != owner[h])
            def _():
                here = piece(att, p, slice(h * HEAD, (h + 1) * HEAD))
                pltpu.make_async_copy(here, here, back_recv.at[p, h]).wait()

    def share(tokens, c):
        return jnp.dot(
            tokens, weight[:, c * width : (c + 1) * width], preferred_element_type=jnp.float32
        )

    def project(p):
        returned(p)
        if p < 2:
            tokens = jnp.concatenate(
                [att[2 * (1 - row) + who, p] for who in (1 - core, core)], axis=0
            )
        else:
            tokens = att[2 * row + (1 - core if p == 2 else core)].reshape(block, heads * HEAD)
        for c in range(chunks):
            part = share(tokens, c)
            if p < 2:
                send_a[p, c, :slab] = part[:slab].astype(jnp.bfloat16)
                own[p, c] = part[slab:]
            elif p == 2:
                send_a[p, c] = part.astype(jnp.bfloat16)
            if p < 3:
                give_a(p, c).start()
            else:
                give_a(2, c).wait_recv()
                part = part + recv_a[2, c].astype(jnp.float32)
                for half_block in range(2):
                    lines = slice(half_block * slab, (half_block + 1) * slab)
                    give_b(half_block, c).wait_recv()
                    out_ref[lines, c * width : (c + 1) * width] = (
                        part[lines] + recv_b[half_block, c].astype(jnp.float32)
                    ).astype(jnp.bfloat16)

    def pair(p):
        for c in range(chunks):
            give_a(p, c).wait_recv()
            send_b[p, c] = (own[p, c] + recv_a[p, c, :slab].astype(jnp.float32)).astype(
                jnp.bfloat16
            )
            give_b(p, c).start()

    def work(p):
        @pl.when(both)
        def _():
            arrive(1, p)

        @pl.when(jnp.logical_not(both))
        def _():
            arrive(0, p)

        @pl.when(core == 0)
        def _():
            if p + ahead < pieces:
                more(p + ahead)

        @pl.when(core == 1)
        def _():
            if p + 1 < pieces:
                more(p + 1)

        @pl.when(both)
        def _():
            attend(1, second, p)
            arrive(0, p)

        attend(0, first, p)

    work(0)
    work(1)
    load_weight.wait()
    project(0)
    work(2)
    pair(0)
    project(1)
    pair(1)
    work(3)
    project(2)
    project(3)

    for c in range(chunks):
        for p in range(3):
            give_a(p, c).wait_send()
        for p in range(2):
            give_b(p, c).wait_send()
    for h in range(heads):

        @pl.when(frame != owner[h])
        def _():
            for a in range(2 + pieces):
                outgoing(h, a).wait_send()

    for i in range(n):

        @pl.when(i != frame)
        def _():
            for p in range(pieces):
                returning(0, first, p, i).wait_send()

        @pl.when(jnp.logical_and(both, i != frame))
        def _():
            for p in range(pieces):
                returning(1, second, p, i).wait_send()


def fused(n, queries, keys, values, band_table, windows, out_weight):
    length, width = queries.shape[1:]
    columns = out_weight.shape[1]
    heads = width // HEAD
    block = length // 4
    slab = block // 2
    chunks = 2
    pieces = 4
    part = columns // chunks
    anywhere = pl.BlockSpec(memory_space=pl.ANY)
    dma = pltpu.SemaphoreType.DMA
    arrays = (queries.reshape(4, 2, slab, width), keys, values, band_table, windows, out_weight)
    mixed = pl.pallas_call(
        functools.partial(fused_kernel, n, chunks),
        out_shape=pltpu.VMEM((block, columns), jnp.bfloat16),
        in_specs=[anywhere] * 6,
        out_specs=pl.BlockSpec(memory_space=pltpu.VMEM),
        scratch_shapes=[
            pltpu.SMEM(band_table.shape, jnp.int32),
            pltpu.SMEM(windows.shape, jnp.int32),
            pltpu.VMEM((2, pieces, n, 2, slab, HEAD), jnp.bfloat16),
            pltpu.VMEM((2, 2, n, length, HEAD), jnp.bfloat16),
            pltpu.VMEM(out_weight.shape, jnp.bfloat16),
            pltpu.VMEM((2, pieces, n, 2, slab, HEAD), jnp.bfloat16),
            pltpu.VMEM((4, 2, slab, width), jnp.bfloat16),
            pltpu.VMEM((3, chunks, block, part), jnp.bfloat16),
            pltpu.VMEM((3, chunks, block, part), jnp.bfloat16),
            pltpu.VMEM((2, chunks, slab, part), jnp.bfloat16),
            pltpu.VMEM((2, chunks, slab, part), jnp.bfloat16),
            pltpu.VMEM((2, chunks, slab, part), jnp.float32),
            pltpu.SemaphoreType.REGULAR((n,)),
            dma((heads, 2 + pieces)),
            dma((2, 2 + pieces, n)),
            dma((2, pieces, n)),
            dma((pieces, heads)),
            dma((3, chunks)),
            dma((3, chunks)),
            dma((2, chunks)),
            dma((2, chunks)),
            dma,
            dma((2,)),
        ],
        compiler_params=pltpu.CompilerParams(
            collective_id=0, has_side_effects=True, vmem_limit_bytes=60 * 1024 * 1024
        ),
    )(*[pltpu.with_memory_space_constraint(x, pltpu.HBM) for x in arrays])
    return mixed[None]


def solution(mesh):
    n = mesh.shape["tm"]

    def step(queries, keys, values, band_table, windows, out_weight):
        paired = mesh.shape["head"] == 2 and mesh.shape["sub"] == 2
        fits = queries.shape[0] == 1 and queries.shape[1] % 128 == 0
        if n > 2 and paired and fits and queries.shape[2] == (2 * n - 2) * HEAD:
            return fused(n, queries, keys, values, band_table, windows, out_weight)
        return local(queries, keys, values, band_table, windows, out_weight)

    return jax.shard_map(
        step,
        mesh=mesh,
        in_specs=(
            P(("clip", "tm"), None, ("head", "sub")),
            P(("clip", "tm"), None, ("head", "sub")),
            P(("clip", "tm"), None, ("head", "sub")),
            P(),
            P(),
            P(("head", "sub"), None),
        ),
        out_specs=P(("clip", "tm"), ("head", "sub"), None),
        check_vma=False,
    )
```

```python
import functools
import math

import jax
import jax.numpy as jnp
from jax import lax
from jax.experimental import pallas as pl
from jax.experimental.pallas import tpu as pltpu
from jax.sharding import PartitionSpec as P

HEAD = 128
MESH = pl.DeviceIdType.MESH


def local(queries, keys, values, band_table, windows, out_weight):
    frames, length, width = queries.shape
    heads = width // HEAD
    scale = HEAD ** (-0.5)
    here = lax.axis_index("tm") * frames
    query = queries[0].reshape(length, heads, HEAD)
    places = lax.iota(jnp.int32, length)
    gap = jnp.abs(places[:, None] - places[None, :])

    def absorb(carry, key_frame, value_frame, frame, usable):
        peak, total, numer = carry
        reach = windows[band_table[here, frame]]
        allowed = (gap <= reach)[None] & usable
        scores = (
            jnp.einsum(
                "phd,qhd->hpq",
                query,
                key_frame.reshape(length, heads, HEAD),
                preferred_element_type=jnp.float32,
            )
            * scale
        )
        masked = jnp.where(allowed, scores, jnp.float32(-1e30))
        top = jnp.maximum(peak, jnp.max(masked, axis=-1))
        weights = jnp.where(allowed, jnp.exp(scores - top[:, :, None]), jnp.float32(0.0))
        shrink = jnp.exp(peak - top)
        total = total * shrink + jnp.sum(weights, axis=-1)
        added = jnp.einsum(
            "hpq,qhd->phd",
            weights.astype(jnp.bfloat16),
            value_frame.reshape(length, heads, HEAD),
            preferred_element_type=jnp.float32,
        )
        numer = numer * jnp.transpose(shrink)[:, :, None] + added
        return (top, total, numer)

    carry = (
        jnp.full((heads, length), -1e30, jnp.float32),
        jnp.zeros((heads, length), jnp.float32),
        jnp.zeros((length, heads, HEAD), jnp.float32),
    )
    skipped = -1
    state = carry
    key_part = lax.all_gather(keys, "tm", axis=0, tiled=True)
    value_part = lax.all_gather(values, "tm", axis=0, tiled=True)

    def advance(inner, item):
        key_frame, value_frame, offset = item
        usable = jnp.abs(offset - here) > skipped
        return (absorb(inner, key_frame, value_frame, offset, usable), None)

    state, unused = lax.scan(
        advance, state, (key_part, value_part, lax.iota(jnp.int32, key_part.shape[0]))
    )
    carry = state
    peak, total, numer = carry
    attended = (
        (numer / jnp.transpose(total)[:, :, None]).astype(jnp.bfloat16).reshape(length, width)
    )
    mixed = lax.psum_scatter(
        jnp.dot(attended, out_weight, preferred_element_type=jnp.float32).astype(jnp.bfloat16),
        ("head", "sub"),
        scatter_dimension=0,
        tiled=True,
    )
    return mixed[None]


def fused_kernel(
    n, chunks, q_hbm, k_hbm, v_hbm, band_hbm, windows_hbm, w_hbm, out_ref,
    band, windows, asked, buf, weight, done, att, send_a, recv_a, send_b, recv_b, own, known,
    in_send, in_pair, in_piece, back_send, back_recv, a_send, a_recv, b_send, b_recv, w_sem, table_sem,
):
    frame = lax.axis_index("tm")
    row = lax.axis_index("head")
    core = lax.axis_index("sub")
    length = k_hbm.shape[1]
    block = length // 4
    slab = block // 2
    pieces = 4
    heads = 2 * n - 2
    half = n // 2
    owner = [(h + 1) // 2 for h in range(heads)]
    slot = [1 if h > 0 and h % 2 == 0 else 0 for h in range(heads)]
    factor = HEAD ** (-0.5) * math.log2(math.e)
    ahead = 2

    def inner(z):
        return z + 1 if z < half else z - 1

    def outward(z):
        return list(range(z - 1, -1, -1)) if z < half else list(range(z + 1, n))

    def beyond(z):
        return list(range(z + 2, n)) if z < half else list(range(z - 2, -1, -1))

    def owned(z):
        return [h for h in range(heads) if owner[h] == z and slot[h]] + [
            h for h in range(heads) if owner[h] == z and not slot[h]
        ]

    def piece(ref, p, columns):
        if p < 2:
            return ref.at[pl.ds(2 * (1 - row), 2), p, :, columns]
        return ref.at[2 * row + (1 - core if p == 2 else core), :, :, columns]

    def ends(h, a):
        columns = slice(h * HEAD, (h + 1) * HEAD)
        if a < 2:
            return (k_hbm, v_hbm)[a].at[0, :, columns], buf.at[slot[h], a, frame]
        return piece(q_hbm, a - 2, columns), asked.at[slot[h], a - 2, frame]

    def landing(h, a):
        return in_pair.at[slot[h]] if a < 2 else in_piece.at[slot[h], a - 2]

    def outgoing(h, a):
        source, target = ends(h, a)
        return pltpu.make_async_remote_copy(
            src_ref=source,
            dst_ref=target,
            send_sem=in_send.at[h],
            recv_sem=landing(h, a),
            device_id={"tm": owner[h]},
            device_id_type=MESH,
        )

    def give(some):
        for h in some:
            for a in range(2):
                outgoing(h, a).start()

    def ask(z, p):
        near = [inner(z)] if z in (half - 1, half) else []
        far = [inner(z)] if z not in (half - 1, half) else []
        for w in near + beyond(z) + far + outward(z):
            for h in owned(w):
                outgoing(h, 2 + p).start()

    def tell(z, w):
        pl.semaphore_signal(known.at[w], inc=1, device_id={"tm": z}, device_id_type=MESH)

    def enter(z):
        barrier = pltpu.get_barrier_semaphore()
        middle = z in (half - 1, half)
        out = outward(z)
        for w in ([inner(z)] if middle else []) + out[:1]:
            pl.semaphore_signal(barrier, inc=1, device_id={"tm": w}, device_id_type=MESH)
        pl.semaphore_signal(barrier, inc=1, device_id={"head": 1 - row}, device_id_type=MESH)
        pl.semaphore_signal(barrier, inc=1, device_id={"sub": 1 - core}, device_id_type=MESH)
        pl.semaphore_wait(barrier, 3)
        if not middle:
            tell(inner(z), z)
        close = owned(inner(z))
        if middle:
            give(close)
        else:
            outgoing(close[0], 0).start()
        for w in out:
            pl.semaphore_wait(known.at[w], 1)
            tell(inner(z), w)
            if w == out[0]:
                tell(w, inner(z))
            give(owned(w))
        for w in beyond(z):
            pl.semaphore_wait(known.at[w], 1)
            if out:
                tell(out[0], w)
            give(owned(w))
        if not middle:
            outgoing(close[0], 1).start()
            give(close[1:])
        ask(z, 0)

        @pl.when(core == 0)
        def _():
            for p in range(1, ahead):
                ask(z, p)

        for h in owned(z):
            for a in range(2 + pieces):
                source, target = ends(h, a)
                pltpu.make_async_copy(source, target, landing(h, a)).start()

    for z in range(n):
        @pl.when(frame == z)
        def _():
            enter(z)

    load_weight = pltpu.make_async_copy(w_hbm, weight, w_sem)
    load_weight.start()
    tables = (
        pltpu.make_async_copy(band_hbm, band, table_sem.at[0]),
        pltpu.make_async_copy(windows_hbm, windows, table_sem.at[1]),
    )
    for table in tables:
        table.start()
    for table in tables:
        table.wait()

    def returning(s, h, p, i):
        return pltpu.make_async_remote_copy(
            src_ref=done.at[s, p, i],
            dst_ref=piece(att, p, pl.ds(pl.multiple_of(h * HEAD, HEAD), HEAD)),
            send_sem=back_send.at[s],
            recv_sem=back_recv.at[p],
            device_id={"tm": i},
            device_id_type=MESH,
        )

    def weigh(s, query, masked):
        scores = []
        for j in range(n):
            score = lax.dot_general(
                query, buf[s, 0, j], (((1,), (1,)), ((), ())), preferred_element_type=jnp.float32
            )
            scores.append(masked(j, score))
        top = scores[0]
        for score in scores[1:]:
            top = jnp.maximum(top, score)
        top = jnp.max(top, axis=-1, keepdims=True)
        total = None
        numer = None
        for j in range(n):
            part = jnp.exp2((scores[j] - top) * factor)
            product = jnp.dot(
                part.astype(jnp.bfloat16), buf[s, 1, j], preferred_element_type=jnp.float32
            )
            total = part if total is None else total + part
            numer = product if numer is None else numer + product
        return (numer / jnp.sum(total, axis=-1, keepdims=True)).astype(jnp.bfloat16)

    second = 2 * frame
    first = 2 * frame - (frame + n - 1) // n
    both = jnp.logical_and(frame > 0, frame < n - 1)
    height = 2 * slab
    line = lax.broadcasted_iota(jnp.int32, (height, length), 0)
    column = lax.broadcasted_iota(jnp.int32, (height, length), 1)

    def away(p):
        if p < 2:
            spot = (line // slab) * block + lax.rem(line, slab)
            start = 2 * (1 - row) * block + p * slab
        else:
            spot = line
            start = (2 * row + (1 - core if p == 2 else core)) * block
        return jnp.abs(spot - column + start)

    def more(p):
        for z in range(n):
            @pl.when(frame == z)
            def _():
                ask(z, p)

    def wait_for(here, sem):
        pltpu.make_async_copy(here, here, sem).wait()

    def arrive(s, p):
        if p == 0:
            wait_for(buf.at[s], in_pair.at[s])
        wait_for(asked.at[s, p], in_piece.at[s, p])

    def attend(s, h, p):
        gap = away(p)

        def masked(j, score):
            return jnp.concatenate(
                [
                    jnp.where(
                        gap <= windows[band[i, j]],
                        score[i * height : (i + 1) * height],
                        jnp.float32(-1e30),
                    )
                    for i in range(n)
                ],
                axis=0,
            )

        result = weigh(s, asked[s, p].reshape(n * height, HEAD), masked)
        for i in range(n):
            mine = result[i * height : (i + 1) * height].reshape(2, slab, HEAD)

            @pl.when(i != frame)
            def _():
                done[s, p, i] = mine
                returning(s, h, p, i).start()

            @pl.when(i == frame)
            def _():
                piece(att, p, pl.ds(pl.multiple_of(h * HEAD, HEAD), HEAD))[...] = mine

    width = weight.shape[1] // chunks

    def give_a(p, c):
        lines = slice(0, slab if p < 2 else block)
        return pltpu.make_async_remote_copy(
            src_ref=send_a.at[p, c, lines], dst_ref=recv_a.at[p, c, lines],
            send_sem=a_send, recv_sem=a_recv.at[p, c],
            device_id={"sub": 1 - core}, device_id_type=MESH,
        )

    def give_b(p, c):
        return pltpu.make_async_remote_copy(
            src_ref=send_b.at[p, c], dst_ref=recv_b.at[p, c],
            send_sem=b_send, recv_sem=b_recv.at[p, c],
            device_id={"head": 1 - row}, device_id_type=MESH,
        )

    def returned(p):
        @pl.when(both)
        def _():
            wait_for(piece(att, p, slice(0, (heads - 2) * HEAD)), back_recv.at[p])

        @pl.when(jnp.logical_not(both))
        def _():
            wait_for(piece(att, p, slice(0, (heads - 1) * HEAD)), back_recv.at[p])

    def share(tokens, c):
        return jnp.dot(
            tokens, weight[:, c * width : (c + 1) * width], preferred_element_type=jnp.float32
        )

    def project(p):
        returned(p)
        if p < 2:
            tokens = jnp.concatenate(
                [att[2 * (1 - row) + who, p] for who in (1 - core, core)], axis=0
            )
        else:
            tokens = att[2 * row + (1 - core if p == 2 else core)].reshape(block, heads * HEAD)
        for c in range(chunks):
            part = share(tokens, c)
            if p < 2:
                send_a[p, c, :slab] = part[:slab].astype(jnp.bfloat16)
                own[p, c] = part[slab:]
            elif p == 2:
                send_a[p, c] = part.astype(jnp.bfloat16)
            if p < 3:
                give_a(p, c).start()
            else:
                give_a(2, c).wait_recv()
                part = part + recv_a[2, c].astype(jnp.float32)
                for half_block in range(2):
                    lines = slice(half_block * slab, (half_block + 1) * slab)
                    give_b(half_block, c).wait_recv()
                    out_ref[lines, c * width : (c + 1) * width] = (
                        part[lines] + recv_b[half_block, c].astype(jnp.float32)
                    ).astype(jnp.bfloat16)

    def pair(p):
        for c in range(chunks):
            give_a(p, c).wait_recv()
            send_b[p, c] = (own[p, c] + recv_a[p, c, :slab].astype(jnp.float32)).astype(
                jnp.bfloat16
            )
            give_b(p, c).start()

    def work(p):
        @pl.when(both)
        def _():
            arrive(1, p)

        @pl.when(jnp.logical_not(both))
        def _():
            arrive(0, p)

        @pl.when(core == 0)
        def _():
            if p + ahead < pieces:
                more(p + ahead)

        @pl.when(core == 1)
        def _():
            if p + 1 < pieces:
                more(p + 1)

        @pl.when(both)
        def _():
            attend(1, second, p)
            arrive(0, p)

        attend(0, first, p)

    work(0)
    work(1)
    load_weight.wait()
    project(0)
    work(2)
    pair(0)
    project(1)
    pair(1)
    work(3)
    project(2)
    project(3)

    wait_for(send_a.at[0:2], a_send)
    wait_for(send_b, b_send)
    for h in range(heads):

        @pl.when(frame != owner[h])
        def _():
            wait_for(buf.at[0, 0, 0:3], in_send.at[h])

    wait_for(done.at[0, :, : n - 1], back_send.at[0])

    @pl.when(both)
    def _():
        wait_for(done.at[1, :, : n - 1], back_send.at[1])


def fused(n, queries, keys, values, band_table, windows, out_weight):
    length, width = queries.shape[1:]
    columns = out_weight.shape[1]
    heads = width // HEAD
    block = length // 4
    slab = block // 2
    chunks = 2
    pieces = 4
    part = columns // chunks
    anywhere = pl.BlockSpec(memory_space=pl.ANY)
    dma = pltpu.SemaphoreType.DMA
    arrays = (queries.reshape(4, 2, slab, width), keys, values, band_table, windows, out_weight)
    mixed = pl.pallas_call(
        functools.partial(fused_kernel, n, chunks),
        out_shape=pltpu.VMEM((block, columns), jnp.bfloat16),
        in_specs=[anywhere] * 6,
        out_specs=pl.BlockSpec(memory_space=pltpu.VMEM),
        scratch_shapes=[
            pltpu.SMEM(band_table.shape, jnp.int32),
            pltpu.SMEM(windows.shape, jnp.int32),
            pltpu.VMEM((2, pieces, n, 2, slab, HEAD), jnp.bfloat16),
            pltpu.VMEM((2, 2, n, length, HEAD), jnp.bfloat16),
            pltpu.VMEM(out_weight.shape, jnp.bfloat16),
            pltpu.VMEM((2, pieces, n, 2, slab, HEAD), jnp.bfloat16),
            pltpu.VMEM((4, 2, slab, width), jnp.bfloat16),
            pltpu.VMEM((3, chunks, block, part), jnp.bfloat16),
            pltpu.VMEM((3, chunks, block, part), jnp.bfloat16),
            pltpu.VMEM((2, chunks, slab, part), jnp.bfloat16),
            pltpu.VMEM((2, chunks, slab, part), jnp.bfloat16),
            pltpu.VMEM((2, chunks, slab, part), jnp.float32),
            pltpu.SemaphoreType.REGULAR((n,)),
            dma((heads,)),
            dma((2,)),
            dma((2, pieces)),
            dma((2,)),
            dma((pieces,)),
            dma,
            dma((3, chunks)),
            dma,
            dma((2, chunks)),
            dma,
            dma((2,)),
        ],
        compiler_params=pltpu.CompilerParams(
            collective_id=0, has_side_effects=True, vmem_limit_bytes=60 * 1024 * 1024
        ),
    )(*[pltpu.with_memory_space_constraint(x, pltpu.HBM) for x in arrays])
    return mixed[None]


def solution(mesh):
    n = mesh.shape["tm"]

    def step(queries, keys, values, band_table, windows, out_weight):
        paired = mesh.shape["head"] == 2 and mesh.shape["sub"] == 2
        fits = queries.shape[0] == 1 and queries.shape[1] % 128 == 0
        if n > 2 and paired and fits and queries.shape[2] == (2 * n - 2) * HEAD:
            return fused(n, queries, keys, values, band_table, windows, out_weight)
        return local(queries, keys, values, band_table, windows, out_weight)

    return jax.shard_map(
        step,
        mesh=mesh,
        in_specs=(
            P(("clip", "tm"), None, ("head", "sub")),
            P(("clip", "tm"), None, ("head", "sub")),
            P(("clip", "tm"), None, ("head", "sub")),
            P(),
            P(),
            P(("head", "sub"), None),
        ),
        out_specs=P(("clip", "tm"), ("head", "sub"), None),
        check_vma=False,
    )
```

```python
import functools
import math

import jax
import jax.numpy as jnp
from jax import lax
from jax.experimental import pallas as pl
from jax.experimental.pallas import tpu as pltpu
from jax.sharding import PartitionSpec as P

HEAD = 128
MESH = pl.DeviceIdType.MESH


def local(queries, keys, values, band_table, windows, out_weight):
    frames, length, width = queries.shape
    heads = width // HEAD
    scale = HEAD ** (-0.5)
    here = lax.axis_index("tm") * frames
    query = queries[0].reshape(length, heads, HEAD)
    places = lax.iota(jnp.int32, length)
    gap = jnp.abs(places[:, None] - places[None, :])

    def absorb(carry, key_frame, value_frame, frame, usable):
        peak, total, numer = carry
        reach = windows[band_table[here, frame]]
        allowed = (gap <= reach)[None] & usable
        scores = (
            jnp.einsum(
                "phd,qhd->hpq",
                query,
                key_frame.reshape(length, heads, HEAD),
                preferred_element_type=jnp.float32,
            )
            * scale
        )
        masked = jnp.where(allowed, scores, jnp.float32(-1e30))
        top = jnp.maximum(peak, jnp.max(masked, axis=-1))
        weights = jnp.where(allowed, jnp.exp(scores - top[:, :, None]), jnp.float32(0.0))
        shrink = jnp.exp(peak - top)
        total = total * shrink + jnp.sum(weights, axis=-1)
        added = jnp.einsum(
            "hpq,qhd->phd",
            weights.astype(jnp.bfloat16),
            value_frame.reshape(length, heads, HEAD),
            preferred_element_type=jnp.float32,
        )
        numer = numer * jnp.transpose(shrink)[:, :, None] + added
        return (top, total, numer)

    carry = (
        jnp.full((heads, length), -1e30, jnp.float32),
        jnp.zeros((heads, length), jnp.float32),
        jnp.zeros((length, heads, HEAD), jnp.float32),
    )
    skipped = -1
    state = carry
    key_part = lax.all_gather(keys, "tm", axis=0, tiled=True)
    value_part = lax.all_gather(values, "tm", axis=0, tiled=True)

    def advance(inner, item):
        key_frame, value_frame, offset = item
        usable = jnp.abs(offset - here) > skipped
        return (absorb(inner, key_frame, value_frame, offset, usable), None)

    state, unused = lax.scan(
        advance, state, (key_part, value_part, lax.iota(jnp.int32, key_part.shape[0]))
    )
    carry = state
    peak, total, numer = carry
    attended = (
        (numer / jnp.transpose(total)[:, :, None]).astype(jnp.bfloat16).reshape(length, width)
    )
    mixed = lax.psum_scatter(
        jnp.dot(attended, out_weight, preferred_element_type=jnp.float32).astype(jnp.bfloat16),
        ("head", "sub"),
        scatter_dimension=0,
        tiled=True,
    )
    return mixed[None]


def fused_kernel(
    n, chunks, q_hbm, k_hbm, v_hbm, band_hbm, windows_hbm, w_hbm, out_ref,
    band, windows, asked, buf, weight, done, att, send_a, recv_a, send_b, recv_b, own, known,
    in_send, in_pair, in_piece, back_send, back_recv, a_send, a_recv, b_send, b_recv, w_sem, table_sem,
):
    frame = lax.axis_index("tm")
    row = lax.axis_index("head")
    core = lax.axis_index("sub")
    length = k_hbm.shape[1]
    block = length // 4
    slab = block // 2
    pieces = 4
    heads = 2 * n - 2
    half = n // 2
    owner = [(h + 1) // 2 for h in range(heads)]
    slot = [1 if h > 0 and h % 2 == 0 else 0 for h in range(heads)]
    factor = HEAD ** (-0.5) * math.log2(math.e)
    ahead = 2

    def inner(z):
        return z + 1 if z < half else z - 1

    def outward(z):
        return list(range(z - 1, -1, -1)) if z < half else list(range(z + 1, n))

    def beyond(z):
        return list(range(z + 2, n)) if z < half else list(range(z - 2, -1, -1))

    def owned(z):
        return [h for h in range(heads) if owner[h] == z and slot[h]] + [
            h for h in range(heads) if owner[h] == z and not slot[h]
        ]

    def piece(ref, p, columns):
        if p < 2:
            return ref.at[pl.ds(2 * (1 - row), 2), p, :, columns]
        return ref.at[2 * row + (1 - core if p == 2 else core), :, :, columns]

    def ends(h, a):
        columns = slice(h * HEAD, (h + 1) * HEAD)
        if a < 2:
            return (k_hbm, v_hbm)[a].at[0, :, columns], buf.at[slot[h], a, frame]
        return piece(q_hbm, a - 2, columns), asked.at[slot[h], a - 2, frame]

    def landing(h, a):
        return in_pair.at[slot[h]] if a < 2 else in_piece.at[slot[h], a - 2]

    def outgoing(h, a):
        source, target = ends(h, a)
        return pltpu.make_async_remote_copy(
            src_ref=source,
            dst_ref=target,
            send_sem=in_send.at[h],
            recv_sem=landing(h, a),
            device_id={"tm": owner[h]},
            device_id_type=MESH,
        )

    def give(some):
        for h in some:
            for a in range(2):
                outgoing(h, a).start()

    def ask(z, p):
        near = [inner(z)] if z in (half - 1, half) else []
        far = [inner(z)] if z not in (half - 1, half) else []
        for w in near + beyond(z) + far + outward(z):
            for h in owned(w):
                outgoing(h, 2 + p).start()

    def tell(z, w):
        pl.semaphore_signal(known.at[w], inc=1, device_id={"tm": z}, device_id_type=MESH)

    def enter(z):
        barrier = pltpu.get_barrier_semaphore()
        middle = z in (half - 1, half)
        out = outward(z)
        for w in ([inner(z)] if middle else []) + out[:1]:
            pl.semaphore_signal(barrier, inc=1, device_id={"tm": w}, device_id_type=MESH)
        pl.semaphore_signal(barrier, inc=1, device_id={"head": 1 - row}, device_id_type=MESH)
        pl.semaphore_signal(barrier, inc=1, device_id={"sub": 1 - core}, device_id_type=MESH)
        pl.semaphore_wait(barrier, 3)
        if not middle:
            tell(inner(z), z)
        close = owned(inner(z))
        if middle:
            give(close)
        else:
            outgoing(close[0], 0).start()
        for w in out:
            pl.semaphore_wait(known.at[w], 1)
            tell(inner(z), w)
            if w == out[0]:
                tell(w, inner(z))
            give(owned(w))
        for w in beyond(z):
            pl.semaphore_wait(known.at[w], 1)
            if out:
                tell(out[0], w)
            give(owned(w))
        if not middle:
            outgoing(close[0], 1).start()
            give(close[1:])
        ask(z, 0)

        @pl.when(core == 0)
        def _():
            for p in range(1, 2 if middle else 2):
                ask(z, p)

        @pl.when(core == 1)
        def _():
            for p in range(1, 1 if middle else 1):
                ask(z, p)

        for h in owned(z):
            for a in range(2 + pieces):
                source, target = ends(h, a)
                pltpu.make_async_copy(source, target, landing(h, a)).start()

    for z in range(n):
        @pl.when(frame == z)
        def _():
            enter(z)

    load_weight = pltpu.make_async_copy(w_hbm, weight, w_sem)
    load_weight.start()
    tables = (
        pltpu.make_async_copy(band_hbm, band, table_sem.at[0]),
        pltpu.make_async_copy(windows_hbm, windows, table_sem.at[1]),
    )
    for table in tables:
        table.start()
    for table in tables:
        table.wait()

    def returning(s, h, p, i):
        return pltpu.make_async_remote_copy(
            src_ref=done.at[s, p, i],
            dst_ref=piece(att, p, pl.ds(pl.multiple_of(h * HEAD, HEAD), HEAD)),
            send_sem=back_send.at[s],
            recv_sem=back_recv.at[p],
            device_id={"tm": i},
            device_id_type=MESH,
        )

    def weigh(s, query, masked):
        scores = []
        for j in range(n):
            score = lax.dot_general(
                query, buf[s, 0, j], (((1,), (1,)), ((), ())), preferred_element_type=jnp.float32
            )
            scores.append(masked(j, score))
        top = scores[0]
        for score in scores[1:]:
            top = jnp.maximum(top, score)
        top = jnp.max(top, axis=-1, keepdims=True)
        total = None
        numer = None
        for j in range(n):
            part = jnp.exp2((scores[j] - top) * factor)
            product = jnp.dot(
                part.astype(jnp.bfloat16), buf[s, 1, j], preferred_element_type=jnp.float32
            )
            total = part if total is None else total + part
            numer = product if numer is None else numer + product
        return (numer / jnp.sum(total, axis=-1, keepdims=True)).astype(jnp.bfloat16)

    second = 2 * frame
    first = 2 * frame - (frame + n - 1) // n
    both = jnp.logical_and(frame > 0, frame < n - 1)
    height = 2 * slab
    line = lax.broadcasted_iota(jnp.int32, (height, length), 0)
    column = lax.broadcasted_iota(jnp.int32, (height, length), 1)

    def away(p):
        if p < 2:
            spot = (line // slab) * block + lax.rem(line, slab)
            start = 2 * (1 - row) * block + p * slab
        else:
            spot = line
            start = (2 * row + (1 - core if p == 2 else core)) * block
        return jnp.abs(spot - column + start)

    def more(p):
        for z in range(n):
            @pl.when(frame == z)
            def _():
                ask(z, p)

    def wait_for(here, sem):
        pltpu.make_async_copy(here, here, sem).wait()

    def arrive(s, p):
        if p == 0:
            wait_for(buf.at[s], in_pair.at[s])
        wait_for(asked.at[s, p], in_piece.at[s, p])

    def attend(s, h, p):
        gap = away(p)

        def masked(j, score):
            return jnp.concatenate(
                [
                    jnp.where(
                        gap <= windows[band[i, j]],
                        score[i * height : (i + 1) * height],
                        jnp.float32(-1e30),
                    )
                    for i in range(n)
                ],
                axis=0,
            )

        result = weigh(s, asked[s, p].reshape(n * height, HEAD), masked)
        for i in range(n):
            mine = result[i * height : (i + 1) * height].reshape(2, slab, HEAD)

            @pl.when(i != frame)
            def _():
                done[s, p, i] = mine
                returning(s, h, p, i).start()

            @pl.when(i == frame)
            def _():
                piece(att, p, pl.ds(pl.multiple_of(h * HEAD, HEAD), HEAD))[...] = mine

    width = weight.shape[1] // chunks

    def give_a(p, c):
        lines = slice(0, slab if p < 2 else block)
        return pltpu.make_async_remote_copy(
            src_ref=send_a.at[p, c, lines], dst_ref=recv_a.at[p, c, lines],
            send_sem=a_send, recv_sem=a_recv.at[p, c],
            device_id={"sub": 1 - core}, device_id_type=MESH,
        )

    def give_b(p, c):
        return pltpu.make_async_remote_copy(
            src_ref=send_b.at[p, c], dst_ref=recv_b.at[p, c],
            send_sem=b_send, recv_sem=b_recv.at[p, c],
            device_id={"head": 1 - row}, device_id_type=MESH,
        )

    def returned(p):
        @pl.when(both)
        def _():
            wait_for(piece(att, p, slice(0, (heads - 2) * HEAD)), back_recv.at[p])

        @pl.when(jnp.logical_not(both))
        def _():
            wait_for(piece(att, p, slice(0, (heads - 1) * HEAD)), back_recv.at[p])

    def share(tokens, c):
        return jnp.dot(
            tokens, weight[:, c * width : (c + 1) * width], preferred_element_type=jnp.float32
        )

    def project(p):
        returned(p)
        if p < 2:
            tokens = jnp.concatenate(
                [att[2 * (1 - row) + who, p] for who in (1 - core, core)], axis=0
            )
        else:
            tokens = att[2 * row + (1 - core if p == 2 else core)].reshape(block, heads * HEAD)
        for c in range(chunks):
            part = share(tokens, c)
            if p < 2:
                send_a[p, c, :slab] = part[:slab].astype(jnp.bfloat16)
                own[p, c] = part[slab:]
            elif p == 2:
                send_a[p, c] = part.astype(jnp.bfloat16)
            if p < 3:
                give_a(p, c).start()
            else:
                give_a(2, c).wait_recv()
                part = part + recv_a[2, c].astype(jnp.float32)
                for half_block in range(2):
                    lines = slice(half_block * slab, (half_block + 1) * slab)
                    give_b(half_block, c).wait_recv()
                    out_ref[lines, c * width : (c + 1) * width] = (
                        part[lines] + recv_b[half_block, c].astype(jnp.float32)
                    ).astype(jnp.bfloat16)

    def pair(p):
        for c in range(chunks):
            give_a(p, c).wait_recv()
            send_b[p, c] = (own[p, c] + recv_a[p, c, :slab].astype(jnp.float32)).astype(
                jnp.bfloat16
            )
            give_b(p, c).start()

    def work(p):
        @pl.when(both)
        def _():
            arrive(1, p)

        @pl.when(jnp.logical_not(both))
        def _():
            arrive(0, p)

        if p + 2 < pieces:

            @pl.when((core == 0) & both)
            def _():
                more(p + 2)

        if p + 1 < pieces:

            @pl.when((core == 1) & both)
            def _():
                more(p + 1)

        if p + 1 < pieces:

            @pl.when((core == 1) & jnp.logical_not(both))
            def _():
                more(p + 1)

        @pl.when(both)
        def _():
            attend(1, second, p)
            arrive(0, p)

        attend(0, first, p)

        if p + 2 < pieces:

            @pl.when((core == 0) & jnp.logical_not(both))
            def _():
                more(p + 2)

    work(0)
    work(1)
    load_weight.wait()
    project(0)
    work(2)
    pair(0)
    project(1)
    pair(1)
    work(3)
    project(2)
    project(3)

    wait_for(send_a.at[0:2], a_send)
    wait_for(send_b, b_send)
    for h in range(heads):

        @pl.when(frame != owner[h])
        def _():
            wait_for(buf.at[0, 0, 0:3], in_send.at[h])

    wait_for(done.at[0, :, : n - 1], back_send.at[0])

    @pl.when(both)
    def _():
        wait_for(done.at[1, :, : n - 1], back_send.at[1])


def fused(n, queries, keys, values, band_table, windows, out_weight):
    length, width = queries.shape[1:]
    columns = out_weight.shape[1]
    heads = width // HEAD
    block = length // 4
    slab = block // 2
    chunks = 2
    pieces = 4
    part = columns // chunks
    anywhere = pl.BlockSpec(memory_space=pl.ANY)
    dma = pltpu.SemaphoreType.DMA
    arrays = (queries.reshape(4, 2, slab, width), keys, values, band_table, windows, out_weight)
    mixed = pl.pallas_call(
        functools.partial(fused_kernel, n, chunks),
        out_shape=pltpu.VMEM((block, columns), jnp.bfloat16),
        in_specs=[anywhere] * 6,
        out_specs=pl.BlockSpec(memory_space=pltpu.VMEM),
        scratch_shapes=[
            pltpu.SMEM(band_table.shape, jnp.int32),
            pltpu.SMEM(windows.shape, jnp.int32),
            pltpu.VMEM((2, pieces, n, 2, slab, HEAD), jnp.bfloat16),
            pltpu.VMEM((2, 2, n, length, HEAD), jnp.bfloat16),
            pltpu.VMEM(out_weight.shape, jnp.bfloat16),
            pltpu.VMEM((2, pieces, n, 2, slab, HEAD), jnp.bfloat16),
            pltpu.VMEM((4, 2, slab, width), jnp.bfloat16),
            pltpu.VMEM((3, chunks, block, part), jnp.bfloat16),
            pltpu.VMEM((3, chunks, block, part), jnp.bfloat16),
            pltpu.VMEM((2, chunks, slab, part), jnp.bfloat16),
            pltpu.VMEM((2, chunks, slab, part), jnp.bfloat16),
            pltpu.VMEM((2, chunks, slab, part), jnp.float32),
            pltpu.SemaphoreType.REGULAR((n,)),
            dma((heads,)),
            dma((2,)),
            dma((2, pieces)),
            dma((2,)),
            dma((pieces,)),
            dma,
            dma((3, chunks)),
            dma,
            dma((2, chunks)),
            dma,
            dma((2,)),
        ],
        compiler_params=pltpu.CompilerParams(
            collective_id=0, has_side_effects=True, vmem_limit_bytes=60 * 1024 * 1024
        ),
    )(*[pltpu.with_memory_space_constraint(x, pltpu.HBM) for x in arrays])
    return mixed[None]


def solution(mesh):
    n = mesh.shape["tm"]

    def step(queries, keys, values, band_table, windows, out_weight):
        paired = mesh.shape["head"] == 2 and mesh.shape["sub"] == 2
        fits = queries.shape[0] == 1 and queries.shape[1] % 128 == 0
        if n > 2 and paired and fits and queries.shape[2] == (2 * n - 2) * HEAD:
            return fused(n, queries, keys, values, band_table, windows, out_weight)
        return local(queries, keys, values, band_table, windows, out_weight)

    return jax.shard_map(
        step,
        mesh=mesh,
        in_specs=(
            P(("clip", "tm"), None, ("head", "sub")),
            P(("clip", "tm"), None, ("head", "sub")),
            P(("clip", "tm"), None, ("head", "sub")),
            P(),
            P(),
            P(("head", "sub"), None),
        ),
        out_specs=P(("clip", "tm"), ("head", "sub"), None),
        check_vma=False,
    )
```

```python
import functools
import math

import jax
import jax.numpy as jnp
from jax import lax
from jax.experimental import pallas as pl
from jax.experimental.pallas import tpu as pltpu
from jax.sharding import PartitionSpec as P

HEAD = 128
MESH = pl.DeviceIdType.MESH


def local(queries, keys, values, band_table, windows, out_weight):
    frames, length, width = queries.shape
    heads = width // HEAD
    scale = HEAD ** (-0.5)
    here = lax.axis_index("tm") * frames
    query = queries[0].reshape(length, heads, HEAD)
    places = lax.iota(jnp.int32, length)
    gap = jnp.abs(places[:, None] - places[None, :])

    def absorb(carry, key_frame, value_frame, frame, usable):
        peak, total, numer = carry
        reach = windows[band_table[here, frame]]
        allowed = (gap <= reach)[None] & usable
        scores = (
            jnp.einsum(
                "phd,qhd->hpq",
                query,
                key_frame.reshape(length, heads, HEAD),
                preferred_element_type=jnp.float32,
            )
            * scale
        )
        masked = jnp.where(allowed, scores, jnp.float32(-1e30))
        top = jnp.maximum(peak, jnp.max(masked, axis=-1))
        weights = jnp.where(allowed, jnp.exp(scores - top[:, :, None]), jnp.float32(0.0))
        shrink = jnp.exp(peak - top)
        total = total * shrink + jnp.sum(weights, axis=-1)
        added = jnp.einsum(
            "hpq,qhd->phd",
            weights.astype(jnp.bfloat16),
            value_frame.reshape(length, heads, HEAD),
            preferred_element_type=jnp.float32,
        )
        numer = numer * jnp.transpose(shrink)[:, :, None] + added
        return (top, total, numer)

    carry = (
        jnp.full((heads, length), -1e30, jnp.float32),
        jnp.zeros((heads, length), jnp.float32),
        jnp.zeros((length, heads, HEAD), jnp.float32),
    )
    skipped = -1
    state = carry
    key_part = lax.all_gather(keys, "tm", axis=0, tiled=True)
    value_part = lax.all_gather(values, "tm", axis=0, tiled=True)

    def advance(inner, item):
        key_frame, value_frame, offset = item
        usable = jnp.abs(offset - here) > skipped
        return (absorb(inner, key_frame, value_frame, offset, usable), None)

    state, unused = lax.scan(
        advance, state, (key_part, value_part, lax.iota(jnp.int32, key_part.shape[0]))
    )
    carry = state
    peak, total, numer = carry
    attended = (
        (numer / jnp.transpose(total)[:, :, None]).astype(jnp.bfloat16).reshape(length, width)
    )
    mixed = lax.psum_scatter(
        jnp.dot(attended, out_weight, preferred_element_type=jnp.float32).astype(jnp.bfloat16),
        ("head", "sub"),
        scatter_dimension=0,
        tiled=True,
    )
    return mixed[None]


def fused_kernel(
    n, chunks, q_hbm, k_hbm, v_hbm, band_hbm, windows_hbm, w_hbm, out_ref,
    band, windows, asked, buf, weight, done, att, send_a, recv_a, send_b, recv_b, own, known,
    in_send, in_pair, in_piece, back_send, back_recv, a_send, a_recv, b_send, b_recv, w_sem, table_sem,
):
    frame = lax.axis_index("tm")
    row = lax.axis_index("head")
    core = lax.axis_index("sub")
    length = k_hbm.shape[1]
    block = length // 4
    slab = block // 2
    pieces = 4
    heads = 2 * n - 2
    half = n // 2
    owner = [(h + 1) // 2 for h in range(heads)]
    slot = [1 if h > 0 and h % 2 == 0 else 0 for h in range(heads)]
    factor = HEAD ** (-0.5) * math.log2(math.e)
    ahead = 2

    def inner(z):
        return z + 1 if z < half else z - 1

    def outward(z):
        return list(range(z - 1, -1, -1)) if z < half else list(range(z + 1, n))

    def beyond(z):
        return list(range(z + 2, n)) if z < half else list(range(z - 2, -1, -1))

    def owned(z):
        return [h for h in range(heads) if owner[h] == z and slot[h]] + [
            h for h in range(heads) if owner[h] == z and not slot[h]
        ]

    def piece(ref, p, columns):
        if p < 2:
            return ref.at[pl.ds(2 * (1 - row), 2), p, :, columns]
        return ref.at[2 * row + (1 - core if p == 2 else core), :, :, columns]

    def ends(h, a):
        columns = slice(h * HEAD, (h + 1) * HEAD)
        if a < 2:
            return (k_hbm, v_hbm)[a].at[0, :, columns], buf.at[slot[h], a, frame]
        return piece(q_hbm, a - 2, columns), asked.at[slot[h], a - 2, frame]

    def landing(h, a):
        return in_pair.at[slot[h]] if a < 2 else in_piece.at[slot[h], a - 2]

    def outgoing(h, a):
        source, target = ends(h, a)
        return pltpu.make_async_remote_copy(
            src_ref=source,
            dst_ref=target,
            send_sem=in_send.at[h],
            recv_sem=landing(h, a),
            device_id={"tm": owner[h]},
            device_id_type=MESH,
        )

    def give(some):
        for h in some:
            for a in range(2):
                outgoing(h, a).start()

    def ask(z, p):
        near = [inner(z)] if z in (half - 1, half) else []
        far = [inner(z)] if z not in (half - 1, half) else []
        for w in near + beyond(z) + far + outward(z):
            for h in owned(w):
                outgoing(h, 2 + p).start()

    def tell(z, w):
        pl.semaphore_signal(known.at[w], inc=1, device_id={"tm": z}, device_id_type=MESH)

    def enter(z):
        barrier = pltpu.get_barrier_semaphore()
        middle = z in (half - 1, half)
        out = outward(z)
        for w in ([inner(z)] if middle else []) + out[:1]:
            pl.semaphore_signal(barrier, inc=1, device_id={"tm": w}, device_id_type=MESH)
        pl.semaphore_signal(barrier, inc=1, device_id={"head": 1 - row}, device_id_type=MESH)
        pl.semaphore_signal(barrier, inc=1, device_id={"sub": 1 - core}, device_id_type=MESH)
        pl.semaphore_wait(barrier, 3)
        if not middle:
            tell(inner(z), z)
        close = owned(inner(z))
        if middle:
            give(close)
        else:
            outgoing(close[0], 0).start()
        for w in out:
            pl.semaphore_wait(known.at[w], 1)
            tell(inner(z), w)
            if w == out[0]:
                tell(w, inner(z))
            give(owned(w))
        for w in beyond(z):
            pl.semaphore_wait(known.at[w], 1)
            if out:
                tell(out[0], w)
            give(owned(w))
        if not middle:
            outgoing(close[0], 1).start()
            give(close[1:])
        ask(z, 0)

        @pl.when(core == 0)
        def _():
            for p in range(1, 2 if middle else 2):
                ask(z, p)

        @pl.when(core == 1)
        def _():
            for p in range(1, 1 if middle else 1):
                ask(z, p)

        for h in owned(z):
            for a in range(2 + pieces):
                source, target = ends(h, a)
                pltpu.make_async_copy(source, target, landing(h, a)).start()

    for z in range(n):
        @pl.when(frame == z)
        def _():
            enter(z)

    load_weight = pltpu.make_async_copy(w_hbm, weight, w_sem)
    load_weight.start()
    tables = (
        pltpu.make_async_copy(band_hbm, band, table_sem.at[0]),
        pltpu.make_async_copy(windows_hbm, windows, table_sem.at[1]),
    )
    for table in tables:
        table.start()
    for table in tables:
        table.wait()

    def distant(h, i):
        return (h >= heads - 2 if i < half else h < 2).astype(jnp.int32)

    def returning(s, h, p, i):
        return pltpu.make_async_remote_copy(
            src_ref=done.at[s, p, i],
            dst_ref=piece(att, p, pl.ds(pl.multiple_of(h * HEAD, HEAD), HEAD)),
            send_sem=back_send.at[s],
            recv_sem=back_recv.at[p if p < pieces - 1 else p + distant(h, i)],
            device_id={"tm": i},
            device_id_type=MESH,
        )

    def weigh(s, query, masked):
        scores = []
        for j in range(n):
            score = lax.dot_general(
                query, buf[s, 0, j], (((1,), (1,)), ((), ())), preferred_element_type=jnp.float32
            )
            scores.append(masked(j, score))
        top = scores[0]
        for score in scores[1:]:
            top = jnp.maximum(top, score)
        top = jnp.max(top, axis=-1, keepdims=True)
        total = None
        numer = None
        for j in range(n):
            part = jnp.exp2((scores[j] - top) * factor)
            product = jnp.dot(
                part.astype(jnp.bfloat16), buf[s, 1, j], preferred_element_type=jnp.float32
            )
            total = part if total is None else total + part
            numer = product if numer is None else numer + product
        return (numer / jnp.sum(total, axis=-1, keepdims=True)).astype(jnp.bfloat16)

    second = 2 * frame
    first = 2 * frame - (frame + n - 1) // n
    both = jnp.logical_and(frame > 0, frame < n - 1)
    height = 2 * slab
    line = lax.broadcasted_iota(jnp.int32, (height, length), 0)
    column = lax.broadcasted_iota(jnp.int32, (height, length), 1)

    def away(p):
        if p < 2:
            spot = (line // slab) * block + lax.rem(line, slab)
            start = 2 * (1 - row) * block + p * slab
        else:
            spot = line
            start = (2 * row + (1 - core if p == 2 else core)) * block
        return jnp.abs(spot - column + start)

    def more(p):
        for z in range(n):
            @pl.when(frame == z)
            def _():
                ask(z, p)

    def wait_for(here, sem):
        pltpu.make_async_copy(here, here, sem).wait()

    def arrive(s, p):
        if p == 0:
            wait_for(buf.at[s], in_pair.at[s])
        wait_for(asked.at[s, p], in_piece.at[s, p])

    def attend(s, h, p):
        gap = away(p)

        def masked(j, score):
            return jnp.concatenate(
                [
                    jnp.where(
                        gap <= windows[band[i, j]],
                        score[i * height : (i + 1) * height],
                        jnp.float32(-1e30),
                    )
                    for i in range(n)
                ],
                axis=0,
            )

        result = weigh(s, asked[s, p].reshape(n * height, HEAD), masked)
        for i in range(n):
            mine = result[i * height : (i + 1) * height].reshape(2, slab, HEAD)

            @pl.when(i != frame)
            def _():
                done[s, p, i] = mine
                returning(s, h, p, i).start()

            @pl.when(i == frame)
            def _():
                piece(att, p, pl.ds(pl.multiple_of(h * HEAD, HEAD), HEAD))[...] = mine

    width = weight.shape[1] // chunks

    def give_a(p, c):
        lines = slice(0, slab if p < 2 else block)
        return pltpu.make_async_remote_copy(
            src_ref=send_a.at[p, c, lines], dst_ref=recv_a.at[p, c, lines],
            send_sem=a_send, recv_sem=a_recv.at[p, c],
            device_id={"sub": 1 - core}, device_id_type=MESH,
        )

    def give_b(p, c):
        return pltpu.make_async_remote_copy(
            src_ref=send_b.at[p, c], dst_ref=recv_b.at[p, c],
            send_sem=b_send, recv_sem=b_recv.at[p, c],
            device_id={"head": 1 - row}, device_id_type=MESH,
        )

    def returned(p):
        @pl.when(both)
        def _():
            wait_for(piece(att, p, slice(0, (heads - 2) * HEAD)), back_recv.at[p])

        @pl.when(jnp.logical_not(both))
        def _():
            wait_for(piece(att, p, slice(0, (heads - 1) * HEAD)), back_recv.at[p])

    def share(tokens, c):
        return jnp.dot(
            tokens, weight[:, c * width : (c + 1) * width], preferred_element_type=jnp.float32
        )

    def project(p):
        returned(p)
        if p < 2:
            tokens = jnp.concatenate(
                [att[2 * (1 - row) + who, p] for who in (1 - core, core)], axis=0
            )
        else:
            tokens = att[2 * row + 1 - core].reshape(block, heads * HEAD)
        for c in range(chunks):
            part = share(tokens, c)
            if p < 2:
                send_a[p, c, :slab] = part[:slab].astype(jnp.bfloat16)
                own[p, c] = part[slab:]
            else:
                send_a[p, c] = part.astype(jnp.bfloat16)
            give_a(p, c).start()

    def conclude():
        p = pieces - 1

        def gathered(heads_here, sem):
            wait_for(piece(att, p, slice(0, heads_here * HEAD)), sem)

        def term(first_head, span, c):
            lanes = pl.ds(pl.multiple_of(first_head * HEAD, 2 * HEAD), span * HEAD)
            return jnp.dot(
                att[2 * row + core, :, :, lanes].reshape(block, span * HEAD),
                weight[lanes, c * width : (c + 1) * width],
                preferred_element_type=jnp.float32,
            )

        @pl.when(both)
        def _():
            gathered(heads - 4, back_recv.at[p])

        @pl.when(jnp.logical_not(both))
        def _():
            gathered(heads - 3, back_recv.at[p])

        low = frame < half
        for c in range(chunks):
            part = term(jnp.where(low, 0, 2), heads - 2, c)
            give_a(2, c).wait_recv()
            part = part + recv_a[2, c].astype(jnp.float32)
            for half_block in range(2):
                own[half_block, c] = part[half_block * slab : (half_block + 1) * slab]
        gathered(2, back_recv.at[p + 1])
        for c in range(chunks):
            part = term(jnp.where(low, heads - 2, 0), 2, c)
            for half_block in range(2):
                lines = slice(half_block * slab, (half_block + 1) * slab)
                give_b(half_block, c).wait_recv()
                out_ref[lines, c * width : (c + 1) * width] = (
                    own[half_block, c] + part[lines] + recv_b[half_block, c].astype(jnp.float32)
                ).astype(jnp.bfloat16)

    def pair(p):
        for c in range(chunks):
            give_a(p, c).wait_recv()
            send_b[p, c] = (own[p, c] + recv_a[p, c, :slab].astype(jnp.float32)).astype(
                jnp.bfloat16
            )
            give_b(p, c).start()

    def work(p):
        @pl.when(both)
        def _():
            arrive(1, p)

        @pl.when(jnp.logical_not(both))
        def _():
            arrive(0, p)

        if p + 2 < pieces:

            @pl.when((core == 0) & both)
            def _():
                more(p + 2)

        if p + 1 < pieces:

            @pl.when((core == 1) & both)
            def _():
                more(p + 1)

        if p + 1 < pieces:

            @pl.when((core == 1) & jnp.logical_not(both))
            def _():
                more(p + 1)

        @pl.when(both)
        def _():
            attend(1, second, p)
            arrive(0, p)

        attend(0, first, p)

        if p + 2 < pieces:

            @pl.when((core == 0) & jnp.logical_not(both))
            def _():
                more(p + 2)

    work(0)
    work(1)
    load_weight.wait()
    project(0)
    work(2)
    pair(0)

    @pl.when(frame == n - 1)
    def _():
        work(3)

    project(1)
    pair(1)

    @pl.when(jnp.logical_not(frame == n - 1))
    def _():
        work(3)

    project(2)
    conclude()

    wait_for(send_a.at[0:2], a_send)
    wait_for(send_b, b_send)
    for h in range(heads):

        @pl.when(frame != owner[h])
        def _():
            wait_for(buf.at[0, 0, 0:3], in_send.at[h])

    wait_for(done.at[0, :, : n - 1], back_send.at[0])

    @pl.when(both)
    def _():
        wait_for(done.at[1, :, : n - 1], back_send.at[1])


def fused(n, queries, keys, values, band_table, windows, out_weight):
    length, width = queries.shape[1:]
    columns = out_weight.shape[1]
    heads = width // HEAD
    block = length // 4
    slab = block // 2
    chunks = 2
    pieces = 4
    part = columns // chunks
    anywhere = pl.BlockSpec(memory_space=pl.ANY)
    dma = pltpu.SemaphoreType.DMA
    arrays = (queries.reshape(4, 2, slab, width), keys, values, band_table, windows, out_weight)
    mixed = pl.pallas_call(
        functools.partial(fused_kernel, n, chunks),
        out_shape=pltpu.VMEM((block, columns), jnp.bfloat16),
        in_specs=[anywhere] * 6,
        out_specs=pl.BlockSpec(memory_space=pltpu.VMEM),
        scratch_shapes=[
            pltpu.SMEM(band_table.shape, jnp.int32),
            pltpu.SMEM(windows.shape, jnp.int32),
            pltpu.VMEM((2, pieces, n, 2, slab, HEAD), jnp.bfloat16),
            pltpu.VMEM((2, 2, n, length, HEAD), jnp.bfloat16),
            pltpu.VMEM(out_weight.shape, jnp.bfloat16),
            pltpu.VMEM((2, pieces, n, 2, slab, HEAD), jnp.bfloat16),
            pltpu.VMEM((4, 2, slab, width), jnp.bfloat16),
            pltpu.VMEM((3, chunks, block, part), jnp.bfloat16),
            pltpu.VMEM((3, chunks, block, part), jnp.bfloat16),
            pltpu.VMEM((2, chunks, slab, part), jnp.bfloat16),
            pltpu.VMEM((2, chunks, slab, part), jnp.bfloat16),
            pltpu.VMEM((2, chunks, slab, part), jnp.float32),
            pltpu.SemaphoreType.REGULAR((n,)),
            dma((heads,)),
            dma((2,)),
            dma((2, pieces)),
            dma((2,)),
            dma((pieces + 1,)),
            dma,
            dma((3, chunks)),
            dma,
            dma((2, chunks)),
            dma,
            dma((2,)),
        ],
        compiler_params=pltpu.CompilerParams(
            collective_id=0, has_side_effects=True, vmem_limit_bytes=60 * 1024 * 1024
        ),
    )(*[pltpu.with_memory_space_constraint(x, pltpu.HBM) for x in arrays])
    return mixed[None]


def solution(mesh):
    n = mesh.shape["tm"]

    def step(queries, keys, values, band_table, windows, out_weight):
        paired = mesh.shape["head"] == 2 and mesh.shape["sub"] == 2
        fits = queries.shape[0] == 1 and queries.shape[1] % 128 == 0
        if n > 2 and paired and fits and queries.shape[2] == (2 * n - 2) * HEAD:
            return fused(n, queries, keys, values, band_table, windows, out_weight)
        return local(queries, keys, values, band_table, windows, out_weight)

    return jax.shard_map(
        step,
        mesh=mesh,
        in_specs=(
            P(("clip", "tm"), None, ("head", "sub")),
            P(("clip", "tm"), None, ("head", "sub")),
            P(("clip", "tm"), None, ("head", "sub")),
            P(),
            P(),
            P(("head", "sub"), None),
        ),
        out_specs=P(("clip", "tm"), ("head", "sub"), None),
        check_vma=False,
    )
```

```python
import functools
import math

import jax
import jax.numpy as jnp
from jax import lax
from jax.experimental import pallas as pl
from jax.experimental.pallas import tpu as pltpu
from jax.sharding import PartitionSpec as P

HEAD = 128
MESH = pl.DeviceIdType.MESH


def local(queries, keys, values, band_table, windows, out_weight):
    frames, length, width = queries.shape
    heads = width // HEAD
    scale = HEAD ** (-0.5)
    here = lax.axis_index("tm") * frames
    query = queries[0].reshape(length, heads, HEAD)
    places = lax.iota(jnp.int32, length)
    gap = jnp.abs(places[:, None] - places[None, :])

    def absorb(carry, key_frame, value_frame, frame, usable):
        peak, total, numer = carry
        reach = windows[band_table[here, frame]]
        allowed = (gap <= reach)[None] & usable
        scores = (
            jnp.einsum(
                "phd,qhd->hpq",
                query,
                key_frame.reshape(length, heads, HEAD),
                preferred_element_type=jnp.float32,
            )
            * scale
        )
        masked = jnp.where(allowed, scores, jnp.float32(-1e30))
        top = jnp.maximum(peak, jnp.max(masked, axis=-1))
        weights = jnp.where(allowed, jnp.exp(scores - top[:, :, None]), jnp.float32(0.0))
        shrink = jnp.exp(peak - top)
        total = total * shrink + jnp.sum(weights, axis=-1)
        added = jnp.einsum(
            "hpq,qhd->phd",
            weights.astype(jnp.bfloat16),
            value_frame.reshape(length, heads, HEAD),
            preferred_element_type=jnp.float32,
        )
        numer = numer * jnp.transpose(shrink)[:, :, None] + added
        return (top, total, numer)

    carry = (
        jnp.full((heads, length), -1e30, jnp.float32),
        jnp.zeros((heads, length), jnp.float32),
        jnp.zeros((length, heads, HEAD), jnp.float32),
    )
    skipped = -1
    state = carry
    key_part = lax.all_gather(keys, "tm", axis=0, tiled=True)
    value_part = lax.all_gather(values, "tm", axis=0, tiled=True)

    def advance(inner, item):
        key_frame, value_frame, offset = item
        usable = jnp.abs(offset - here) > skipped
        return (absorb(inner, key_frame, value_frame, offset, usable), None)

    state, unused = lax.scan(
        advance, state, (key_part, value_part, lax.iota(jnp.int32, key_part.shape[0]))
    )
    carry = state
    peak, total, numer = carry
    attended = (
        (numer / jnp.transpose(total)[:, :, None]).astype(jnp.bfloat16).reshape(length, width)
    )
    mixed = lax.psum_scatter(
        jnp.dot(attended, out_weight, preferred_element_type=jnp.float32).astype(jnp.bfloat16),
        ("head", "sub"),
        scatter_dimension=0,
        tiled=True,
    )
    return mixed[None]


def fused_kernel(
    n, chunks, q_hbm, k_hbm, v_hbm, band_hbm, windows_hbm, w_hbm, out_ref,
    band, windows, asked, buf, weight, done, att, send_a, recv_a, send_b, recv_b, own, known,
    in_send, in_pair, in_piece, back_send, back_recv, a_send, a_recv, b_send, b_recv, w_sem, table_sem,
):
    frame = lax.axis_index("tm")
    row = lax.axis_index("head")
    core = lax.axis_index("sub")
    length = k_hbm.shape[1]
    block = length // 4
    slab = block // 2
    pieces = 4
    heads = 2 * n - 2
    half = n // 2
    owner = [(h + 1) // 2 for h in range(heads)]
    slot = [1 if h > 0 and h % 2 == 0 else 0 for h in range(heads)]
    factor = HEAD ** (-0.5) * math.log2(math.e)
    ahead = 2

    def inner(z):
        return z + 1 if z < half else z - 1

    def outward(z):
        return list(range(z - 1, -1, -1)) if z < half else list(range(z + 1, n))

    def beyond(z):
        return list(range(z + 2, n)) if z < half else list(range(z - 2, -1, -1))

    def owned(z):
        return [h for h in range(heads) if owner[h] == z and slot[h]] + [
            h for h in range(heads) if owner[h] == z and not slot[h]
        ]

    def piece(ref, p, columns):
        if p < 2:
            return ref.at[pl.ds(2 * (1 - row), 2), p, :, columns]
        return ref.at[2 * row + (1 - core if p == 2 else core), :, :, columns]

    def ends(h, a):
        columns = slice(h * HEAD, (h + 1) * HEAD)
        if a < 2:
            return (k_hbm, v_hbm)[a].at[0, :, columns], buf.at[slot[h], a, frame]
        return piece(q_hbm, a - 2, columns), asked.at[slot[h], a - 2, frame]

    def landing(h, a):
        return in_pair.at[slot[h]] if a < 2 else in_piece.at[slot[h], a - 2]

    def outgoing(h, a):
        source, target = ends(h, a)
        return pltpu.make_async_remote_copy(
            src_ref=source,
            dst_ref=target,
            send_sem=in_send,
            recv_sem=landing(h, a),
            device_id={"tm": owner[h]},
            device_id_type=MESH,
        )

    def give(some):
        for h in some:
            for a in range(2):
                outgoing(h, a).start()

    def ask(z, p):
        near = [inner(z)] if z in (half - 1, half) else []
        far = [inner(z)] if z not in (half - 1, half) else []
        for w in near + beyond(z) + far + outward(z):
            for h in owned(w):
                outgoing(h, 2 + p).start()

    def tell(z, w):
        pl.semaphore_signal(known.at[w], inc=1, device_id={"tm": z}, device_id_type=MESH)

    def enter(z):
        barrier = pltpu.get_barrier_semaphore()
        middle = z in (half - 1, half)
        out = outward(z)
        for w in ([inner(z)] if middle else []) + out[:1]:
            pl.semaphore_signal(barrier, inc=1, device_id={"tm": w}, device_id_type=MESH)
        pl.semaphore_signal(barrier, inc=1, device_id={"head": 1 - row}, device_id_type=MESH)
        pl.semaphore_signal(barrier, inc=1, device_id={"sub": 1 - core}, device_id_type=MESH)
        pl.semaphore_wait(barrier, 3)
        if not middle:
            tell(inner(z), z)
        close = owned(inner(z))
        if middle:
            give(close)
        else:
            outgoing(close[0], 0).start()
        for w in out:
            pl.semaphore_wait(known.at[w], 1)
            tell(inner(z), w)
            if w == out[0]:
                tell(w, inner(z))
            give(owned(w))
        for w in beyond(z):
            pl.semaphore_wait(known.at[w], 1)
            if out:
                tell(out[0], w)
            give(owned(w))
        if not middle:
            outgoing(close[0], 1).start()
            give(close[1:])
        ask(z, 0)

        @pl.when(core == 0)
        def _():
            for p in range(1, 2 if middle else 2):
                ask(z, p)

        @pl.when(core == 1)
        def _():
            for p in range(1, 1 if middle else 1):
                ask(z, p)

        for h in owned(z):
            for a in range(2 + pieces):
                source, target = ends(h, a)
                pltpu.make_async_copy(source, target, landing(h, a)).start()

    for z in range(n):
        @pl.when(frame == z)
        def _():
            enter(z)

    load_weight = pltpu.make_async_copy(w_hbm, weight, w_sem)
    load_weight.start()
    tables = (
        pltpu.make_async_copy(band_hbm, band, table_sem.at[0]),
        pltpu.make_async_copy(windows_hbm, windows, table_sem.at[1]),
    )
    for table in tables:
        table.start()
    for table in tables:
        table.wait()

    def returning(s, h, p, i):
        return pltpu.make_async_remote_copy(
            src_ref=done.at[s, p, i],
            dst_ref=piece(att, p, pl.ds(pl.multiple_of(h * HEAD, HEAD), HEAD)),
            send_sem=back_send.at[s],
            recv_sem=back_recv.at[p],
            device_id={"tm": i},
            device_id_type=MESH,
        )

    def weigh(s, query, masked):
        scores = []
        for j in range(n):
            score = lax.dot_general(
                query, buf[s, 0, j], (((1,), (1,)), ((), ())), preferred_element_type=jnp.float32
            )
            scores.append(masked(j, score))
        top = scores[0]
        for score in scores[1:]:
            top = jnp.maximum(top, score)
        top = jnp.max(top, axis=-1, keepdims=True)
        total = None
        numer = None
        for j in range(n):
            part = jnp.exp2((scores[j] - top) * factor)
            product = jnp.dot(
                part.astype(jnp.bfloat16), buf[s, 1, j], preferred_element_type=jnp.float32
            )
            total = part if total is None else total + part
            numer = product if numer is None else numer + product
        return (numer / jnp.sum(total, axis=-1, keepdims=True)).astype(jnp.bfloat16)

    second = 2 * frame
    first = 2 * frame - (frame + n - 1) // n
    both = jnp.logical_and(frame > 0, frame < n - 1)
    height = 2 * slab
    line = lax.broadcasted_iota(jnp.int32, (height, length), 0)
    column = lax.broadcasted_iota(jnp.int32, (height, length), 1)

    def away(p):
        if p < 2:
            spot = (line // slab) * block + lax.rem(line, slab)
            start = 2 * (1 - row) * block + p * slab
        else:
            spot = line
            start = (2 * row + (1 - core if p == 2 else core)) * block
        return jnp.abs(spot - column + start)

    def more(p):
        for z in range(n):
            @pl.when(frame == z)
            def _():
                ask(z, p)

    def wait_for(here, sem):
        pltpu.make_async_copy(here, here, sem).wait()

    def arrive(s, p):
        if p == 0:
            wait_for(buf.at[s], in_pair.at[s])
        wait_for(asked.at[s, p], in_piece.at[s, p])

    def attend(s, h, p):
        gap = away(p)

        def masked(j, score):
            return jnp.concatenate(
                [
                    jnp.where(
                        gap <= windows[band[i, j]],
                        score[i * height : (i + 1) * height],
                        jnp.float32(-1e30),
                    )
                    for i in range(n)
                ],
                axis=0,
            )

        result = weigh(s, asked[s, p].reshape(n * height, HEAD), masked)
        for i in range(n):
            mine = result[i * height : (i + 1) * height].reshape(2, slab, HEAD)

            @pl.when(i != frame)
            def _():
                done[s, p, i] = mine
                returning(s, h, p, i).start()

            @pl.when(i == frame)
            def _():
                piece(att, p, pl.ds(pl.multiple_of(h * HEAD, HEAD), HEAD))[...] = mine

    width = weight.shape[1] // chunks

    def give_a(p, c):
        lines = slice(0, slab if p < 2 else block)
        return pltpu.make_async_remote_copy(
            src_ref=send_a.at[p, c, lines], dst_ref=recv_a.at[p, c, lines],
            send_sem=a_send, recv_sem=a_recv.at[p, c],
            device_id={"sub": 1 - core}, device_id_type=MESH,
        )

    def give_b(p, c):
        return pltpu.make_async_remote_copy(
            src_ref=send_b.at[p, c], dst_ref=recv_b.at[p, c],
            send_sem=b_send, recv_sem=b_recv.at[p, c],
            device_id={"head": 1 - row}, device_id_type=MESH,
        )

    def returned(p):
        @pl.when(both)
        def _():
            wait_for(piece(att, p, slice(0, (heads - 2) * HEAD)), back_recv.at[p])

        @pl.when(jnp.logical_not(both))
        def _():
            wait_for(piece(att, p, slice(0, (heads - 1) * HEAD)), back_recv.at[p])

    def share(tokens, c):
        return jnp.dot(
            tokens, weight[:, c * width : (c + 1) * width], preferred_element_type=jnp.float32
        )

    def project(p):
        returned(p)
        if p < 2:
            tokens = jnp.concatenate(
                [att[2 * (1 - row) + who, p] for who in (1 - core, core)], axis=0
            )
        else:
            tokens = att[2 * row + (1 - core if p == 2 else core)].reshape(block, heads * HEAD)
        for c in range(chunks):
            part = share(tokens, c)
            if p < 2:
                send_a[p, c, :slab] = part[:slab].astype(jnp.bfloat16)
                own[p, c] = part[slab:]
            elif p == 2:
                send_a[p, c] = part.astype(jnp.bfloat16)
            if p < 3:
                give_a(p, c).start()
            else:
                give_a(2, c).wait_recv()
                part = part + recv_a[2, c].astype(jnp.float32)
                for half_block in range(2):
                    lines = slice(half_block * slab, (half_block + 1) * slab)
                    give_b(half_block, c).wait_recv()
                    out_ref[lines, c * width : (c + 1) * width] = (
                        part[lines] + recv_b[half_block, c].astype(jnp.float32)
                    ).astype(jnp.bfloat16)

    def pair(p):
        for c in range(chunks):
            give_a(p, c).wait_recv()
            send_b[p, c] = (own[p, c] + recv_a[p, c, :slab].astype(jnp.float32)).astype(
                jnp.bfloat16
            )
            give_b(p, c).start()

    def work(p):
        @pl.when(both)
        def _():
            arrive(1, p)

        @pl.when(jnp.logical_not(both))
        def _():
            arrive(0, p)

        if p + 2 < pieces:

            @pl.when((core == 0) & both)
            def _():
                more(p + 2)

        if p + 1 < pieces:

            @pl.when((core == 1) & both)
            def _():
                more(p + 1)

        if p + 1 < pieces:

            @pl.when((core == 1) & jnp.logical_not(both))
            def _():
                more(p + 1)

        @pl.when(both)
        def _():
            attend(1, second, p)
            arrive(0, p)

        attend(0, first, p)

        if p + 2 < pieces:

            @pl.when((core == 0) & jnp.logical_not(both))
            def _():
                more(p + 2)

    work(0)
    work(1)
    load_weight.wait()
    project(0)
    work(2)
    pair(0)
    project(1)
    pair(1)
    work(3)
    project(2)
    project(3)

    wait_for(send_a.at[0:2], a_send)
    wait_for(send_b, b_send)
    sent = 3 * length * HEAD // weight.shape[1]

    @pl.when(both)
    def _():
        wait_for(weight.at[: (heads - 2) * sent], in_send)

    @pl.when(jnp.logical_not(both))
    def _():
        wait_for(weight.at[: (heads - 1) * sent], in_send)

    wait_for(done.at[0, :, : n - 1], back_send.at[0])

    @pl.when(both)
    def _():
        wait_for(done.at[1, :, : n - 1], back_send.at[1])


def fused(n, queries, keys, values, band_table, windows, out_weight):
    length, width = queries.shape[1:]
    columns = out_weight.shape[1]
    heads = width // HEAD
    block = length // 4
    slab = block // 2
    chunks = 2
    pieces = 4
    part = columns // chunks
    anywhere = pl.BlockSpec(memory_space=pl.ANY)
    dma = pltpu.SemaphoreType.DMA
    arrays = (queries.reshape(4, 2, slab, width), keys, values, band_table, windows, out_weight)
    mixed = pl.pallas_call(
        functools.partial(fused_kernel, n, chunks),
        out_shape=pltpu.VMEM((block, columns), jnp.bfloat16),
        in_specs=[anywhere] * 6,
        out_specs=pl.BlockSpec(memory_space=pltpu.VMEM),
        scratch_shapes=[
            pltpu.SMEM(band_table.shape, jnp.int32),
            pltpu.SMEM(windows.shape, jnp.int32),
            pltpu.VMEM((2, pieces, n, 2, slab, HEAD), jnp.bfloat16),
            pltpu.VMEM((2, 2, n, length, HEAD), jnp.bfloat16),
            pltpu.VMEM(out_weight.shape, jnp.bfloat16),
            pltpu.VMEM((2, pieces, n, 2, slab, HEAD), jnp.bfloat16),
            pltpu.VMEM((4, 2, slab, width), jnp.bfloat16),
            pltpu.VMEM((3, chunks, block, part), jnp.bfloat16),
            pltpu.VMEM((3, chunks, block, part), jnp.bfloat16),
            pltpu.VMEM((2, chunks, slab, part), jnp.bfloat16),
            pltpu.VMEM((2, chunks, slab, part), jnp.bfloat16),
            pltpu.VMEM((2, chunks, slab, part), jnp.float32),
            pltpu.SemaphoreType.REGULAR((n,)),
            dma,
            dma((2,)),
            dma((2, pieces)),
            dma((2,)),
            dma((pieces,)),
            dma,
            dma((3, chunks)),
            dma,
            dma((2, chunks)),
            dma,
            dma((2,)),
        ],
        compiler_params=pltpu.CompilerParams(
            collective_id=0, has_side_effects=True, vmem_limit_bytes=60 * 1024 * 1024
        ),
    )(*[pltpu.with_memory_space_constraint(x, pltpu.HBM) for x in arrays])
    return mixed[None]


def solution(mesh):
    n = mesh.shape["tm"]

    def step(queries, keys, values, band_table, windows, out_weight):
        paired = mesh.shape["head"] == 2 and mesh.shape["sub"] == 2
        fits = queries.shape[0] == 1 and queries.shape[1] % 128 == 0
        fits = fits and 3 * queries.shape[1] * HEAD % (8 * out_weight.shape[1]) == 0
        if n > 2 and paired and fits and queries.shape[2] == (2 * n - 2) * HEAD:
            return fused(n, queries, keys, values, band_table, windows, out_weight)
        return local(queries, keys, values, band_table, windows, out_weight)

    return jax.shard_map(
        step,
        mesh=mesh,
        in_specs=(
            P(("clip", "tm"), None, ("head", "sub")),
            P(("clip", "tm"), None, ("head", "sub")),
            P(("clip", "tm"), None, ("head", "sub")),
            P(),
            P(),
            P(("head", "sub"), None),
        ),
        out_specs=P(("clip", "tm"), ("head", "sub"), None),
        check_vma=False,
    )
```
